256 devices in a mesh: dp: 2 (over core), seq: 16 (over x, y), tensor: 8 (over z).
Axes of the slice: x: 4, y: 4, z: 8, core: 2. Of those that a mesh axis runs over, the one named last changes fastest.
Arguments:
- hidden: bfloat16 [16384, 7168], P(('dp', 'seq')), may hold values from -34 to 34
- grad_out: bfloat16 [16384, 4096], P(('dp', 'seq'), 'tensor'), may hold values from -24 to 24
- master_weight: float32 [7168, 4096], P(('dp', 'seq'), 'tensor'), may hold values from -6 to 6
- row_prev: float32 [7168], P(('dp', 'seq')), may hold values from 0.01 to 0.3
- col_prev: float32 [4096], P('tensor'), may hold values from 0.01 to 0.3
Outputs:
- new_weight: bfloat16 [7168, 4096], P('dp', 'tensor')
- update: float32 [7168, 4096], P(('dp', 'seq'), 'tensor')
- new_rows: float32 [7168], P(('dp', 'seq'))
- new_cols: float32 [4096], P('tensor')
The draws below stay inside these ranges and needn't reach their ends.
All inputs are finite; a program needn't handle non-finite values.
Results may differ from the reference program's by a relative error of at most 0.0004.
Values may be sent and summed in bfloat16 or wider, within the bound.
A program may use at most 128 MiB of HBM per device.

```python
import math
import jax
import jax.numpy as jnp
from jax import lax

D = 4096
FF_WIN = 7168
TOKENS = 16384


def hidden_parts(key):
    first, second = jax.random.split(jax.random.fold_in(key, 11), 2)
    ramp = jnp.arange(FF_WIN).astype(jnp.float32) / FF_WIN - 0.5
    unit = jnp.exp(jax.random.uniform(first, (FF_WIN,), minval=-1.15, maxval=1.15)) * jnp.exp(math.log(3.0) * ramp)
    values = jax.random.truncated_normal(second, -4.0, 4.0, (TOKENS, FF_WIN)) * unit
    return (values, unit)


def draw_hidden(key, part):
    values, unit = hidden_parts(key)
    return values.astype(jnp.bfloat16)


def draw_grad_out(key, part):
    values, unit = hidden_parts(key)
    first, second, third = jax.random.split(jax.random.fold_in(key, 23), 3)
    ramp = jnp.arange(D).astype(jnp.float32) / D - 0.5
    column = jnp.exp(jax.random.uniform(first, (D,), minval=-1.15, maxval=1.15)) * jnp.exp(math.log(3.0) * ramp)
    column = column / jnp.sqrt(jnp.float32(TOKENS))
    chosen = jax.random.permutation(third, FF_WIN)[:D]
    carried = values[:, chosen] / unit[chosen][None, :]
    strength = 0.4 * jnp.sqrt(jnp.float32(D) / jnp.float32(TOKENS))
    noise = jax.random.truncated_normal(second, -4.0, 4.0, (TOKENS, D))
    values_out = (0.5 * noise + strength * carried) * column[None, :]
    return values_out.astype(jnp.bfloat16)


def steps_of(key, extent, cuts, least, largest):
    def one(position, blocks):
        heights = jax.random.uniform(jax.random.fold_in(jax.random.fold_in(key, 6), position), (blocks,), jnp.float32, least / len(cuts), largest / len(cuts))
        return jnp.repeat(jnp.exp(heights), extent[position] // blocks).reshape((-1,) + (1,) * (len(extent) - position - 1))

    loudness = one(*cuts[0])
    for cut in cuts[1:]:
        loudness = loudness * one(*cut)
    return loudness


def gaussian(key, dims, spread, bound, shards=(), dtype=jnp.bfloat16):
    result = spread * jax.random.normal(key, dims, jnp.float32)
    if shards:
        result = result * steps_of(key, dims, shards, -0.22, 0.18)
    return jnp.clip(result, -bound, bound).astype(dtype)


def setup_inputs(seed: int = 0) -> dict:
    seeds = jax.random.split(jax.random.key(seed), 6)
    hidden = draw_hidden(jax.random.fold_in(seeds[5], 71), 0)
    grad_out = draw_grad_out(jax.random.fold_in(seeds[5], 71), 0)
    master_weight = gaussian(seeds[2], (FF_WIN, D), 1.0, 6.0, ((0, 32), (1, 8)), jnp.float32)
    row_prev = jnp.clip(jnp.exp(math.log(0.3) - 3.4011974 * jax.random.uniform(seeds[3], (FF_WIN,), jnp.float32) ** steps_of(seeds[3], (FF_WIN,), ((0, 32),), -0.2, 0.2)), 0.01, 0.3)
    col_prev = jnp.clip(jnp.exp(math.log(0.3) - 3.4011974 * jax.random.uniform(seeds[4], (D,), jnp.float32) ** steps_of(seeds[4], (D,), ((0, 8),), -0.2, 0.2)), 0.01, 0.3)
    return dict(hidden=hidden, grad_out=grad_out, master_weight=master_weight, row_prev=row_prev, col_prev=col_prev)


decay_rate = 0.8
learn_rate = 0.05
small_term = 1e-06

def reference(hidden, grad_out, master_weight, row_prev, col_prev):
    grads = lax.dot_general(hidden, grad_out, (((0,), (0,)), ((), ())), preferred_element_type=jnp.float32)
    squares = grads * grads + small_term
    new_rows = decay_rate * row_prev + (1.0 - decay_rate) * lax.optimization_barrier(jnp.sum(squares, axis=1)) / D
    new_cols = decay_rate * col_prev + (1.0 - decay_rate) * lax.optimization_barrier(jnp.sum(squares, axis=0)) / FF_WIN
    second = new_rows[:, None] * new_cols[None, :]
    raw = grads / jnp.sqrt(second)
    size = jnp.sqrt(jnp.sum(raw * raw) / (FF_WIN * D))
    update = raw / jnp.maximum(1.0, size)
    new_weight = (master_weight - learn_rate * update).astype(jnp.bfloat16)
    return (new_weight, update, new_rows, new_cols)
```

```python
import jax
import jax.numpy as jnp
from jax import lax
from jax.experimental import pallas as pl
from jax.experimental.pallas import tpu as pltpu
from jax.sharding import PartitionSpec as P

D = 4096
FF_WIN = 7168
decay_rate = 0.8
learn_rate = 0.05
small_term = 1e-06

N = 4
NZ = 8
TOK = 512
ROWS = 224
COLS = 512
HALF = FF_WIN // 2
CHUNK = HALF // N
H = 128
MSG = ROWS + 16
POWER = 9.0
TOP = 15000.0
OFFS = (2, 1, 3, 0)
MESH = pl.DeviceIdType.MESH


def pick(i, values):
    out = values[-1]
    for n in range(len(values) - 2, -1, -1):
        out = jnp.where(i == n, values[n], out)
    return out


def encode(ref, value):
    groups = value.reshape(ROWS // 16, 16, H)
    peak = jnp.maximum(jnp.max(jnp.abs(groups), axis=0), 1e-30).astype(jnp.bfloat16)
    scale = TOP / peak.astype(jnp.float32)
    u = groups * scale[None]
    u2 = u * u
    u4 = u2 * u2
    u8 = u4 * u4
    ref[pl.ds(0, ROWS), :] = (u8 * u).astype(jnp.bfloat16).reshape(ROWS, H)
    ref[pl.ds(ROWS, 16), :] = peak


def decode(ref):
    code = ref[pl.ds(0, ROWS), :].astype(jnp.float32).reshape(ROWS // 16, 16, H)
    scale = ref[pl.ds(ROWS, 16), :].astype(jnp.float32) * (1.0 / TOP)
    size = jnp.exp(jnp.log(jnp.maximum(jnp.abs(code), 1.2e-38)) * (1.0 / POWER))
    return (size * jnp.where(code < 0.0, -scale[None], scale[None])).reshape(ROWS, H)


def kernel(
    hid, gout, master, rprev, cprev,
    nw, upd_out, nrows_out, ncols_out,
    h_own, h_par, g_own, g_par, part, s1buf, r1buf, s2buf, r2buf, grad, mas, rp, cp,
    rowx, tall, colx, coly, colc, sizx, upd, nrow, ncol,
    ld_sem, xs_sem, xr_sem, s1s, r1s, s2s, r2s, zs, zr, cs, cr, ss, sr, a1s, a1r, a2s, a2r, out_sem,
):
    c = lax.axis_index("dp")
    s = lax.axis_index("seq")
    z = lax.axis_index("tensor")
    x = s // N
    y = s % N

    def wrap(v):
        return lax.rem(v + N, N)

    def at(px, py):
        return (c, wrap(px) * N + wrap(py), z)

    partner = (1 - c, s, z)
    peers_x = [at(x + d, y) for d in range(1, N)]
    peers_y = [at(x, y + d) for d in range(1, N)]
    peers_z = [(c, s, lax.rem(z + d, NZ)) for d in range(1, NZ)]

    barrier = pltpu.get_barrier_semaphore()
    everyone = [partner] + peers_x + peers_y + peers_z
    for peer in everyone:
        pl.semaphore_signal(barrier, inc=1, device_id=peer, device_id_type=MESH)

    def load(src, dst, n):
        copy = pltpu.make_async_copy(src, dst, ld_sem.at[n])
        return copy

    def columns(core, j):
        xi = wrap(x + pick(j, OFFS))
        return pl.ds(pl.multiple_of(core * HALF + xi * CHUNK, 128), CHUNK)

    loads = [load(gout, g_own, 4)]
    loads += [load(hid.at[:, columns(c, j)], h_own.at[j], j) for j in range(N)]
    loads += [load(master, mas, 5), load(rprev, rp, 6), load(cprev, cp, 7)]
    for copy in loads:
        copy.start()
    pl.semaphore_wait(barrier, len(everyone))

    def remote(src, dst, send, recv, peer):
        return pltpu.make_async_remote_copy(
            src_ref=src, dst_ref=dst, send_sem=send, recv_sem=recv, device_id=peer, device_id_type=MESH
        )

    swap_g = remote(gout, g_par, xs_sem.at[4], xr_sem.at[4], partner)
    swap_g.start()

    def swap_h(j):
        return remote(hid.at[:, columns(1 - c, j)], h_par.at[j], xs_sem.at[j], xr_sem.at[j], partner)

    for j in range(N):
        swap_h(j).start()

    right_x, left_x = at(x + 1, y), at(x - 1, y)
    right_y, left_y = at(x, y + 1), at(x, y - 1)
    link1 = [right_x, left_x, right_y, left_y]
    link2 = [right_y, left_y, right_x, left_x]

    def msg1(k, kind, i):
        return remote(s1buf.at[k, kind, i], r1buf.at[k, kind, i], s1s.at[k, kind, i], r1s.at[k, kind, i], link1[k])

    def msg2(k, kind):
        return remote(s2buf.at[k, kind], r2buf.at[k, kind], s2s.at[k, kind], r2s.at[k, kind], link2[k])

    def own(k):
        return pl.ds(k * H, H)

    def other(k):
        return pl.ds((k ^ 1) * H, H)

    def y_of(i):
        return wrap(y + pick(i, OFFS))

    loads[0].wait()
    swap_g.wait_recv()

    def send1(k, kind, i, value):
        encode(s1buf.at[k, kind, i], value)
        msg1(k, kind, i).start()

    def chunk(j, carry):
        load(hid.at[:, columns(c, j)], h_own.at[j], j).wait()
        dims = (((0,), (0,)), ((), ()))
        first = lax.dot_general(h_own[j], g_own[...], dims, preferred_element_type=jnp.float32)
        part[j] = first.reshape(N, ROWS, COLS)
        swap_h(j).wait_recv()
        second = lax.dot_general(h_par[j], g_par[...], dims, preferred_element_type=jnp.float32)
        part[j] += second.reshape(N, ROWS, COLS)

        @pl.when(j == 0)
        def _():
            def body(i, carry):
                for k in (0, 1):
                    send1(k, 0, i, part[0, y_of(i), :, own(k)])
                return carry

            lax.fori_loop(0, N, body, 0)

        for k in (2, 3):
            send1(k, 0, j, part[j, wrap(y + 2), :, own(k)])
        for k in (2, 3):
            send1(k, 1, j, part[j, wrap(y + (1 if k == 2 else -1)), :, other(k)])

        @pl.when(j == 1)
        def _():
            def body(i, carry):
                send1(0, 1, i, part[1, y_of(i), :, other(0)])
                return carry

            lax.fori_loop(0, N, body, 0)

        @pl.when(j == 2)
        def _():
            def body(i, carry):
                send1(1, 1, i, part[2, y_of(i), :, other(1)])
                return carry

            lax.fori_loop(0, N, body, 0)

        return carry

    lax.fori_loop(0, N, chunk, 0)

    def target(k, i):
        if k < 2:
            return part.at[1 + k, y_of(i), :, own(k)]
        return part.at[i, wrap(y + (1 if k == 2 else -1)), :, own(k)]

    def combine(i, carry):
        for k in range(4):
            msg1(k, 0, i).wait_recv()
            send1(k, 2, i, target(k, i)[...] + decode(r1buf.at[k, 0, i]))
        return carry

    lax.fori_loop(0, N, combine, 0)

    def mine(k, i):
        if k < 2:
            return part.at[3, y_of(i), :, own(k)]
        return part.at[i, y, :, own(k)]

    def send2(k, kind, value):
        encode(s2buf.at[k, kind], value)
        msg2(k, kind).start()

    def settle(i, carry):
        for k in range(4):
            msg1(k, 1, i).wait_recv()
            msg1(k, 2, i).wait_recv()
        for k in range(4):
            mine(k, i)[...] += decode(r1buf.at[k, 2, i]) + decode(r1buf.at[k ^ 1, 1, i])

        @pl.when(i == 0)
        def _():
            for k in range(4):
                send2(k, 0, mine(k, 0)[...])

        for step in (0, 1):

            @pl.when(i == 1 + step)
            def _():
                for k in (step, 2 + step):
                    send2(k, 1, mine(k ^ 1, 1 + step)[...])

        return carry

    lax.fori_loop(0, N - 1, settle, 0)
    for k in range(4):
        msg2(k, 0).wait_recv()
        send2(k, 2, mine(k, 1 + (k & 1))[...] + decode(r2buf.at[k, 0]))
    settle(jnp.int32(3), 0)
    for k in range(4):
        msg2(k, 1).wait_recv()
    for k in range(4):
        msg2(k, 2).wait_recv()
    for k in range(4):
        grad[:, own(k)] = mine(k, 3)[...] + decode(r2buf.at[k, 2]) + decode(r2buf.at[k ^ 1, 1])

    g = grad[...]
    squares = g * g + small_term
    folded = squares[:, 0:128] + squares[:, 128:256] + squares[:, 256:384] + squares[:, 384:512]
    tall[pl.ds(0, ROWS), :] = folded
    tall[pl.ds(ROWS, 256 - ROWS), :] = jnp.zeros((256 - ROWS, 128), jnp.float32)
    rowx[z] = jnp.sum(tall[...].T.reshape(16, 8, 256), axis=0)

    def exchange(ref, slot, peers, send, recv):
        copies = [remote(ref.at[slot], ref.at[slot], send.at[n], recv.at[n], peer) for n, peer in enumerate(peers)]
        for copy in copies:
            copy.start()
        for copy in copies:
            copy.wait_recv()
        return copies

    pending = exchange(rowx, z, peers_z, zs, zr)
    loads[6].wait()
    loads[7].wait()
    row_total = jnp.sum(jnp.sum(rowx[...], axis=0), axis=0, keepdims=True)
    new_rows = decay_rate * rp[...] + (1.0 - decay_rate) * row_total[:, 0:ROWS] / D
    nrow[...] = new_rows
    wide = jnp.concatenate([new_rows, jnp.ones((1, 256 - ROWS), jnp.float32)], axis=1)
    row_scale = lax.rsqrt(jnp.broadcast_to(wide, (128, 256)).T[0:ROWS, :])
    scaled = g * jnp.concatenate([row_scale] * 4, axis=1)

    col_sum = jnp.sum(squares, axis=0, keepdims=True)
    col_raw = jnp.sum(scaled * scaled, axis=0, keepdims=True)
    line = lax.broadcasted_iota(jnp.int32, (8, COLS), 0)
    colx[x] = jnp.where(line == 0, col_sum, jnp.where(line == 1, col_raw, 0.0))
    pending += exchange(colx, x, peers_x, cs.at[0], cr.at[0])
    coly[y] = colx[0] + colx[1] + colx[2] + colx[3]
    pending += exchange(coly, y, peers_y, cs.at[1], cr.at[1])
    colc[c] = coly[0] + coly[1] + coly[2] + coly[3]
    pending += exchange(colc, c, [partner], cs.at[2], cr.at[2])
    both = colc[0] + colc[1]
    new_cols = decay_rate * cp[...] + (1.0 - decay_rate) * both[0:1] / FF_WIN
    ncol[...] = new_cols
    ratio = both[1:2] / new_cols
    short = ratio[:, 0:128] + ratio[:, 128:256] + ratio[:, 256:384] + ratio[:, 384:512]
    sizx[z] = jnp.where(lax.broadcasted_iota(jnp.int32, (8, 128), 0) == 0, short, 0.0)
    pending += exchange(sizx, z, peers_z, ss, sr)
    raw_total = jnp.sum(jnp.sum(jnp.sum(sizx[...], axis=0), axis=0, keepdims=True), axis=1, keepdims=True)
    size = jnp.sqrt(raw_total / (FF_WIN * D))
    clip = 1.0 / jnp.maximum(1.0, size)
    update = scaled * (lax.rsqrt(new_cols) * clip)
    loads[5].wait()
    nw[s] = (mas[...] - learn_rate * update).astype(jnp.bfloat16)

    def block(px, py):
        return wrap(px) * N + wrap(py)

    def spread(k):
        return pl.ds((k // 2) * 2 * H, 2 * H)

    def ag(sems, index, src, cols, peer):
        send, recv = sems
        return remote(nw.at[src, :, cols], nw.at[src, :, cols], send.at[index], recv.at[index], peer)

    def source(k, n):
        step = (0, -1, 1, 2)[n]
        return block(x + step, y) if k < 2 else block(x, y + step)

    def first(k):
        return ag((a1s, a1r), (k, 0), s, spread(k), link1[k])

    def first_in(k):
        return ag((a1s, a1r), (k, 0), source(k, 1 + (k & 1)), spread(k), link1[k])

    def relay(k):
        return ag((a1s, a1r), (k, 1), source(k, 1 + (k & 1)), own(k), link1[k])

    def second(k, n):
        return ag((a2s, a2r), (k, n, 0), source(k, n), spread(k), link2[k])

    def beside(k, n):
        step = (0, -1, 1, 2)[n]
        back = -1 if (k & 1) == 0 else 1
        return block(x + step, y + back) if k < 2 else block(x + back, y + step)

    def third(k, n):
        return ag((a2s, a2r), (k, n, 1), beside(k, n), own(k), link2[k])

    sends = []

    def go(copy):
        copy.start()
        sends.append(copy)

    for k in range(4):
        go(first(k))
    for k in range(4):
        go(second(k, 0))
    upd[...] = update
    for k in (0, 2, 1, 3):
        first_in(k).wait_recv()
        go(relay(k))
        pair = k & 2
        go(second(pair, 1 + (k & 1)))
        go(second(pair + 1, 1 + (k & 1)))
    saves = [
        pltpu.make_async_copy(upd, upd_out, out_sem.at[0]),
        pltpu.make_async_copy(nrow, nrows_out, out_sem.at[1]),
        pltpu.make_async_copy(ncol, ncols_out, out_sem.at[2]),
    ]
    for copy in saves:
        copy.start()
    for k in range(4):
        second(k, 0).wait_recv()
        go(third(k, 0))
    for pair in (0, 2):
        for k in (pair, pair + 1):
            relay(k).wait_recv()
        for k in (pair, pair + 1):
            go(second(k, 3))
    for n in (1, 2, 3):
        for k in range(4):
            second(k, n).wait_recv()
            go(third(k, n))
    for n in range(4):
        for k in range(4):
            third(k, n).wait_recv()

    for copy in sends + pending:
        copy.wait_send()
    swap_g.wait_send()
    for j in range(N):
        swap_h(j).wait_send()

    def drain(i, carry):
        for k in range(4):
            for kind in range(3):
                msg1(k, kind, i).wait_send()
        return carry

    lax.fori_loop(0, N, drain, 0)
    for k in range(4):
        for kind in range(3):
            msg2(k, kind).wait_send()
    for copy in saves:
        copy.wait()


def per_device(hidden, grad_out, master_weight, row_prev, col_prev):
    any_space = pl.BlockSpec(memory_space=pl.ANY)
    f32, bf16 = jnp.float32, jnp.bfloat16
    dma = pltpu.SemaphoreType.DMA
    nw, upd, nrows, ncols = pl.pallas_call(
        kernel,
        out_shape=(
            jax.ShapeDtypeStruct((N * N, ROWS, COLS), bf16),
            jax.ShapeDtypeStruct((ROWS, COLS), f32),
            jax.ShapeDtypeStruct((1, ROWS), f32),
            jax.ShapeDtypeStruct((1, COLS), f32),
        ),
        in_specs=[any_space] * 5,
        out_specs=(pl.BlockSpec(memory_space=pltpu.VMEM), any_space, any_space, any_space),
        scratch_shapes=[
            pltpu.VMEM((N, TOK, CHUNK), bf16),
            pltpu.VMEM((N, TOK, CHUNK), bf16),
            pltpu.VMEM((TOK, COLS), bf16),
            pltpu.VMEM((TOK, COLS), bf16),
            pltpu.VMEM((N, N, ROWS, COLS), f32),
            pltpu.VMEM((4, 3, N, MSG, H), bf16),
            pltpu.VMEM((4, 3, N, MSG, H), bf16),
            pltpu.VMEM((4, 3, MSG, H), bf16),
            pltpu.VMEM((4, 3, MSG, H), bf16),
            pltpu.VMEM((ROWS, COLS), f32),
            pltpu.VMEM((ROWS, COLS), f32),
            pltpu.VMEM((1, ROWS), f32),
            pltpu.VMEM((1, COLS), f32),
            pltpu.VMEM((NZ, 8, 256), f32),
            pltpu.VMEM((256, 128), f32),
            pltpu.VMEM((N, 8, COLS), f32),
            pltpu.VMEM((N, 8, COLS), f32),
            pltpu.VMEM((2, 8, COLS), f32),
            pltpu.VMEM((NZ, 8, 128), f32),
            pltpu.VMEM((ROWS, COLS), f32),
            pltpu.VMEM((1, ROWS), f32),
            pltpu.VMEM((1, COLS), f32),
            dma((8,)), dma((5,)), dma((5,)),
            dma((4, 3, N)), dma((4, 3, N)), dma((4, 3)), dma((4, 3)),
            dma((NZ - 1,)), dma((NZ - 1,)), dma((3, 3)), dma((3, 3)), dma((NZ - 1,)), dma((NZ - 1,)),
            dma((4, 2)), dma((4, 2)), dma((4, 4, 2)), dma((4, 4, 2)), dma((3,)),
        ],
        compiler_params=pltpu.CompilerParams(
            collective_id=0, has_side_effects=True, vmem_limit_bytes=60 * 1024 * 1024
        ),
    )(hidden, grad_out, master_weight, row_prev.reshape(1, ROWS), col_prev.reshape(1, COLS))
    return nw.reshape(HALF, COLS), upd, nrows.reshape(ROWS), ncols.reshape(COLS)


def solution(mesh):
    return jax.shard_map(
        per_device,
        mesh=mesh,
        in_specs=(
            P(("dp", "seq"), None),
            P(("dp", "seq"), "tensor"),
            P(("dp", "seq"), "tensor"),
            P(("dp", "seq")),
            P("tensor"),
        ),
        out_specs=(P("dp", "tensor"), P(("dp", "seq"), "tensor"), P(("dp", "seq")), P("tensor")),
        check_vma=False,
    )
```

```python
import jax
import jax.numpy as jnp
from jax import lax
from jax.experimental import pallas as pl
from jax.experimental.pallas import tpu as pltpu
from jax.sharding import PartitionSpec as P

D = 4096
FF_WIN = 7168
decay_rate = 0.8
learn_rate = 0.05
small_term = 1e-06

N = 4
NZ = 8
TOK = 512
ROWS = 224
COLS = 512
HALF = FF_WIN // 2
CHUNK = HALF // N
H = 128
MSG = ROWS + 16
POWER = 9.0
TOP = 15000.0
OFFS = (2, 1, 3, 0)
MESH = pl.DeviceIdType.MESH


def pick(i, values):
    out = values[-1]
    for n in range(len(values) - 2, -1, -1):
        out = jnp.where(i == n, values[n], out)
    return out


def encode(ref, value):
    groups = value.reshape(ROWS // 16, 16, H)
    peak = jnp.maximum(jnp.max(jnp.abs(groups), axis=0), 1e-30).astype(jnp.bfloat16)
    scale = TOP / peak.astype(jnp.float32)
    u = groups * scale[None]
    u2 = u * u
    u4 = u2 * u2
    u8 = u4 * u4
    ref[pl.ds(0, ROWS), :] = (u8 * u).astype(jnp.bfloat16).reshape(ROWS, H)
    ref[pl.ds(ROWS, 16), :] = peak


def decode(ref):
    code = ref[pl.ds(0, ROWS), :].astype(jnp.float32).reshape(ROWS // 16, 16, H)
    scale = ref[pl.ds(ROWS, 16), :].astype(jnp.float32) * (1.0 / TOP)
    size = jnp.exp(jnp.log(jnp.maximum(jnp.abs(code), 1.2e-38)) * (1.0 / POWER))
    return (size * jnp.where(code < 0.0, -scale[None], scale[None])).reshape(ROWS, H)


def kernel(
    hid, gout, master, rprev, cprev,
    nw, upd, nrow, ncol,
    h_own, h_par, g_own, g_par, flat, s1buf, r1buf, s2buf, r2buf, grad, mas, rp, cp,
    rowx, tall, plane, colc, sizx,
    ld_sem, xs_sem, xr_sem, s1s, r1s, s2s, r2s, zs, zr, cs, cr, ps, pr, ss, sr, ws, wr, bs, br, a2s, a2r, chain,
):
    c = lax.axis_index("dp")
    s = lax.axis_index("seq")
    z = lax.axis_index("tensor")
    x = s // N
    y = s % N

    def wrap(v):
        return lax.rem(v + N, N)

    def at(px, py):
        return (c, wrap(px) * N + wrap(py), z)

    partner = (1 - c, s, z)
    peers_plane = [at(x + d // N, y + d % N) for d in range(1, N * N)]
    peers_z = [(c, s, lax.rem(z + d, NZ)) for d in range(1, NZ)]
    right_x, left_x = at(x + 1, y), at(x - 1, y)
    right_y, left_y = at(x, y + 1), at(x, y - 1)
    link1 = [right_x, left_x, right_y, left_y]
    link2 = [right_y, left_y, right_x, left_x]
    near = link1 + [peers_z[0], peers_z[-1]]

    barrier = pltpu.get_barrier_semaphore()
    for peer in [partner] + near:
        pl.semaphore_signal(barrier, inc=1, device_id=peer, device_id_type=MESH)

    first = 1 - y // 2
    near_window = pl.ds(pl.multiple_of(first * 384, 128), 512)
    far_window = pl.ds(pl.multiple_of((1 - first) * 512, 128), 384)

    def start_of(core, j):
        return core * HALF + wrap(x + pick(j, OFFS)) * CHUNK

    def columns(core, j):
        return pl.ds(pl.multiple_of(start_of(core, j), 128), CHUNK)

    def load(src, dst, n):
        return pltpu.make_async_copy(src, dst, ld_sem.at[n])

    def load_h(j):
        return load(hid.at[:, columns(c, j)], h_own.at[j], j)

    load_g = load(gout, g_own, 4)
    small = [load(master, mas, 5), load(rprev, rp, 6), load(cprev, cp, 7)]
    load_g.start()
    for j in range(N):
        load_h(j).start()
    pl.semaphore_wait(barrier, 1 + len(near))

    def remote(src, dst, send, recv, peer):
        return pltpu.make_async_remote_copy(
            src_ref=src, dst_ref=dst, send_sem=send, recv_sem=recv, device_id=peer, device_id_type=MESH
        )

    def tell(n):
        for peer in near:
            pl.semaphore_signal(chain.at[n], inc=1, device_id=peer, device_id_type=MESH)

    def told(n):
        pl.semaphore_wait(chain.at[n], len(near))

    left_half, right_half = pl.ds(0, 2 * H), pl.ds(2 * H, 2 * H)
    base = start_of(1 - c, 0)
    src_near = pl.ds(pl.multiple_of(base + first * 384, 128), 512)
    src_far = pl.ds(pl.multiple_of(base + (1 - first) * 512, 128), 384)

    def swap(n, src, dst):
        return remote(src, dst, xs_sem.at[n], xr_sem.at[n], partner)

    def swap_h(j):
        return swap(j, hid.at[:, columns(1 - c, j)], h_par.at[j])

    swap_near = swap(0, hid.at[:, src_near], h_par.at[0, :, near_window])
    swap_far = swap(6, hid.at[:, src_far], h_par.at[0, :, far_window])
    swap_ga = swap(4, gout.at[:, left_half], g_par.at[:, left_half])
    swap_gb = swap(5, gout.at[:, right_half], g_par.at[:, right_half])
    swaps = [swap_ga, swap_near, swap_far, swap_gb] + [swap_h(j) for j in range(1, N)]
    for copy in swaps:
        copy.start()
    for copy in small:
        copy.start()
    tell(0)

    def msg1(k, kind, i):
        return remote(s1buf.at[k, kind, i], r1buf.at[k, kind, i], s1s.at[k, kind, i], r1s.at[k, kind, i], link1[k])

    def msg2(k, kind):
        return remote(s2buf.at[k, kind], r2buf.at[k, kind], s2s.at[k, kind], r2s.at[k, kind], link2[k])

    def own(k):
        return pl.ds(k * H, H)

    def other(k):
        return pl.ds((k ^ 1) * H, H)

    def y_of(i):
        return pick(i, (wrap(y + 2), wrap(y + 2) + 1 - 2 * (y % 2), y + 1 - 2 * (y % 2), y))

    def part(j, v, cols):
        return flat.at[j, pl.ds(pl.multiple_of(v * ROWS, 32), ROWS), cols]

    def send1(k, kind, i, value):
        encode(s1buf.at[k, kind, i], value)
        msg1(k, kind, i).start()

    dims = (((0,), (0,)), ((), ()))

    def dot(h, g):
        return lax.dot_general(h, g, dims, preferred_element_type=jnp.float32)

    def ahead(k):
        return 1 if (k & 1) == 0 else -1

    def send_b(j):
        for k in (2, 3):
            send1(k, 0, j, part(j, wrap(y + 2), own(k))[...])
        for k in (2, 3):
            send1(k, 1, j, part(j, wrap(y + ahead(k)), other(k))[...])

    def send_a(i, carry):
        for k in (0, 1):
            send1(k, 0, i, part(0, y_of(i), own(k))[...])
        return carry

    load_g.wait()
    load_h(0).wait()
    flat[0] = dot(h_own[0], g_own[...])
    swap_ga.wait_recv()
    swap_near.wait_recv()
    flat[0, near_window, left_half] += dot(h_par[0, :, near_window], g_par[:, left_half])
    lax.fori_loop(0, 2, send_a, 0)
    swap_far.wait_recv()
    flat[0, far_window, left_half] += dot(h_par[0, :, far_window], g_par[:, left_half])
    lax.fori_loop(2, N, send_a, 0)
    swap_gb.wait_recv()
    flat[0, :, right_half] += dot(h_par[0], g_par[:, right_half])
    send_b(0)
    told(0)
    tell(1)

    def chunk(j, carry):
        load_h(j).wait()
        flat[j] = dot(h_own[j], g_own[...])
        swap_h(j).wait_recv()
        flat[j] += dot(h_par[j], g_par[...])
        send_b(j)

        for k in (0, 1):

            @pl.when(j == 1 + k)
            def _():
                def body(i, carry):
                    send1(k, 1, i, part(1 + k, y_of(i), other(k))[...])
                    return carry

                lax.fori_loop(0, N, body, 0)

        return carry

    lax.fori_loop(1, N, chunk, 0)
    told(1)
    tell(2)

    def target(k, i):
        if k < 2:
            return part(1 + k, y_of(i), own(k))
        return part(i, wrap(y + ahead(k)), own(k))

    def combine(i, carry):
        for k in range(4):
            msg1(k, 0, i).wait_recv()
            send1(k, 2, i, target(k, i)[...] + decode(r1buf.at[k, 0, i]))
        return carry

    lax.fori_loop(0, N, combine, 0)

    def mine(k, i):
        if k < 2:
            return part(3, y_of(i), own(k))
        return part(i, y, own(k))

    def beyond(k, cols):
        if k < 2:
            return part(3, wrap(y + ahead(k)), cols)
        return part(1 + (k & 1), y, cols)

    def send2(k, kind, value):
        encode(s2buf.at[k, kind], value)
        msg2(k, kind).start()

    def settle(i, carry):
        for k in range(4):
            msg1(k, 1, i).wait_recv()
            msg1(k, 2, i).wait_recv()
        for k in range(4):
            mine(k, i)[...] += decode(r1buf.at[k, 2, i]) + decode(r1buf.at[k ^ 1, 1, i])

        @pl.when(i == 0)
        def _():
            for k in range(4):
                send2(k, 0, mine(k, 0)[...])

        @pl.when(i == 2)
        def _():
            for k in range(4):
                send2(k, 1, beyond(k, other(k))[...])

        return carry

    lax.fori_loop(0, N - 1, settle, 0)
    for k in range(4):
        msg2(k, 0).wait_recv()
        send2(k, 2, beyond(k, own(k))[...] + decode(r2buf.at[k, 0]))
    settle(jnp.int32(3), 0)
    told(2)
    for k in range(4):
        msg2(k, 1).wait_recv()
    for k in range(4):
        msg2(k, 2).wait_recv()
    for k in range(4):
        grad[:, own(k)] = mine(k, 3)[...] + decode(r2buf.at[k, 2]) + decode(r2buf.at[k ^ 1, 1])

    g = grad[...]
    squares = g * g + small_term
    folded = squares[:, 0:128] + squares[:, 128:256] + squares[:, 256:384] + squares[:, 384:512]
    tall[pl.ds(0, ROWS), :] = folded
    tall[pl.ds(ROWS, 256 - ROWS), :] = jnp.zeros((256 - ROWS, 128), jnp.float32)
    rowx[z] = jnp.sum(tall[...].T.reshape(16, 8, 256), axis=0)

    def exchange(ref, slot, peers, send, recv):
        copies = [remote(ref.at[slot], ref.at[slot], send.at[n], recv.at[n], peer) for n, peer in enumerate(peers)]
        for copy in copies:
            copy.start()
        return copies

    def arrive(copies):
        for copy in copies:
            copy.wait_recv()
        return copies

    pending = exchange(rowx, z, peers_z, zs, zr)
    col_sum = jnp.sum(squares, axis=0, keepdims=True)
    for copy in small:
        copy.wait()
    arrive(pending)
    row_total = jnp.sum(jnp.sum(rowx[...], axis=0), axis=0, keepdims=True)
    new_rows = decay_rate * rp[...] + (1.0 - decay_rate) * row_total[:, 0:ROWS] / D
    nrow[...] = new_rows
    wide = jnp.concatenate([new_rows, jnp.ones((1, 256 - ROWS), jnp.float32)], axis=1)
    row_scale = jnp.broadcast_to(lax.rsqrt(wide), (128, 256)).T[0:ROWS, :]
    scaled = g * jnp.concatenate([row_scale] * 4, axis=1)

    colc[c, pl.ds(0, 1), :] = col_sum
    colc[c, pl.ds(1, 1), :] = jnp.sum(scaled * scaled, axis=0, keepdims=True)
    pending += arrive(exchange(colc, c, [partner], cs, cr))
    plane[s] = colc[0] + colc[1]
    pending += arrive(exchange(plane, s, peers_plane, ps, pr))
    both = jnp.sum(plane[...], axis=0)
    new_cols = decay_rate * cp[...] + (1.0 - decay_rate) * both[0:1] / FF_WIN
    ncol[...] = new_cols
    ratio = both[1:2] / new_cols
    short = ratio[:, 0:128] + ratio[:, 128:256] + ratio[:, 256:384] + ratio[:, 384:512]
    sizx[z] = jnp.where(lax.broadcasted_iota(jnp.int32, (8, 128), 0) == 0, short, 0.0)
    last = exchange(sizx, z, peers_z, ss, sr)
    raw = scaled * lax.rsqrt(new_cols)
    pending += arrive(last)
    raw_total = jnp.sum(jnp.sum(jnp.sum(sizx[...], axis=0), axis=0, keepdims=True), axis=1, keepdims=True)
    size = jnp.sqrt(raw_total / (FF_WIN * D))
    update = raw * (1.0 / jnp.maximum(1.0, size))
    nw[s] = (mas[...] - learn_rate * update).astype(jnp.bfloat16)

    def block(px, py):
        return wrap(px) * N + wrap(py)

    def pair(k):
        return pl.ds((k // 2) * 2 * H, 2 * H)

    def gather(send, recv, src, cols, peer):
        return remote(nw.at[src, :, cols], nw.at[src, :, cols], send, recv, peer)

    from_link = [block(x - 1, y), block(x + 1, y), block(x, y - 1), block(x, y + 1)]
    opposite = [block(x + 2, y), block(x, y + 2)]

    def whole(k, src):
        return gather(ws.at[k], wr.at[k], src, pl.ds(0, COLS), link1[k])

    def relay(k, src):
        return gather(bs.at[k], br.at[k], src, pl.ds((k & 1) * 2 * H, 2 * H), link1[k])

    def second(k, n, src):
        return gather(a2s.at[k, n, 0], a2r.at[k, n, 0], src, pair(k), link2[k])

    def beside(k, n):
        step = (-1, 1, 2)[n]
        return block(x + step, y - ahead(k)) if k < 2 else block(x - ahead(k), y + step)

    def third(k, n):
        return gather(a2s.at[k, n, 1], a2r.at[k, n, 1], beside(k, n), own(k), link2[k])

    sends = []

    def go(copy):
        copy.start()
        sends.append(copy)

    for k in range(4):
        go(whole(k, s))
    upd[...] = update
    for k in (0, 2, 1, 3):
        whole(k, from_link[k]).wait_recv()
        go(relay(k, from_link[k]))
        for side in (0, 1):
            go(second((k & 2) + side, k & 1, from_link[k]))
    for k, axis in ((0, 0), (3, 1)):
        relay(k, opposite[axis]).wait_recv()
        for side in (0, 1):
            go(second(axis * 2 + side, 2, opposite[axis]))
    for n in range(3):
        for k in range(4):
            second(k, n, beside(k, n)).wait_recv()
            go(third(k, n))
    relay(1, opposite[0]).wait_recv()
    relay(2, opposite[1]).wait_recv()
    for n in range(3):
        for k in range(4):
            third(k, n).wait_recv()

    for copy in sends + pending + swaps:
        copy.wait_send()

    def drain(i, carry):
        for k in range(4):
            for kind in range(3):
                msg1(k, kind, i).wait_send()
        return carry

    lax.fori_loop(0, N, drain, 0)
    for k in range(4):
        for kind in range(3):
            msg2(k, kind).wait_send()


def writer(nw, upd, nrow, ncol, nw_out, upd_out, nrow_out, ncol_out, sem):
    quarter = N * N // 4
    pairs = [(nw.at[pl.ds(n * quarter, quarter)], nw_out.at[pl.ds(n * quarter, quarter)]) for n in range(4)]
    pairs += [(upd, upd_out), (nrow, nrow_out), (ncol, ncol_out)]
    copies = [pltpu.make_async_copy(src, dst, sem.at[n]) for n, (src, dst) in enumerate(pairs)]
    for copy in copies:
        copy.start()
    for copy in copies:
        copy.wait()


def per_device(hidden, grad_out, master_weight, row_prev, col_prev):
    hbm = pl.BlockSpec(memory_space=pltpu.HBM)
    vmem = pl.BlockSpec(memory_space=pltpu.VMEM)
    f32, bf16 = jnp.float32, jnp.bfloat16
    dma = pltpu.SemaphoreType.DMA
    results = (((N * N, ROWS, COLS), bf16), ((ROWS, COLS), f32), ((1, ROWS), f32), ((1, COLS), f32))
    held = pl.pallas_call(
        kernel,
        out_shape=tuple(pltpu.VMEM(shape, kind) for shape, kind in results),
        in_specs=[hbm] * 5,
        out_specs=(vmem,) * 4,
        scratch_shapes=[
            pltpu.VMEM((N, TOK, CHUNK), bf16),
            pltpu.VMEM((N, TOK, CHUNK), bf16),
            pltpu.VMEM((TOK, COLS), bf16),
            pltpu.VMEM((TOK, COLS), bf16),
            pltpu.VMEM((N, CHUNK, COLS), f32),
            pltpu.VMEM((4, 3, N, MSG, H), bf16),
            pltpu.VMEM((4, 3, N, MSG, H), bf16),
            pltpu.VMEM((4, 3, MSG, H), bf16),
            pltpu.VMEM((4, 3, MSG, H), bf16),
            pltpu.VMEM((ROWS, COLS), f32),
            pltpu.VMEM((ROWS, COLS), f32),
            pltpu.VMEM((1, ROWS), f32),
            pltpu.VMEM((1, COLS), f32),
            pltpu.VMEM((NZ, 8, 256), f32),
            pltpu.VMEM((256, 128), f32),
            pltpu.VMEM((N * N, 2, COLS), f32),
            pltpu.VMEM((2, 2, COLS), f32),
            pltpu.VMEM((NZ, 8, 128), f32),
            dma((8,)), dma((7,)), dma((7,)),
            dma((4, 3, N)), dma((4, 3, N)), dma((4, 3)), dma((4, 3)),
            dma((NZ - 1,)), dma((NZ - 1,)), dma((1,)), dma((1,)), dma((N * N - 1,)), dma((N * N - 1,)),
            dma((NZ - 1,)), dma((NZ - 1,)),
            dma((4,)), dma((4,)), dma((4,)), dma((4,)), dma((4, 3, 2)), dma((4, 3, 2)),
            pltpu.SemaphoreType.REGULAR((3,)),
        ],
        compiler_params=pltpu.CompilerParams(collective_id=0, has_side_effects=True, vmem_limit_bytes=62700000),
    )(hidden, grad_out, master_weight, row_prev.reshape(1, ROWS), col_prev.reshape(1, COLS))
    nw, upd, nrows, ncols = pl.pallas_call(
        writer,
        out_shape=tuple(jax.ShapeDtypeStruct(shape, kind) for shape, kind in results),
        in_specs=[vmem] * 4,
        out_specs=(hbm,) * 4,
        scratch_shapes=[dma((7,))],
        compiler_params=pltpu.CompilerParams(vmem_limit_bytes=1024 * 1024),
    )(*held)
    return nw.reshape(HALF, COLS), upd, nrows.reshape(ROWS), ncols.reshape(COLS)


def solution(mesh):
    return jax.shard_map(
        per_device,
        mesh=mesh,
        in_specs=(
            P(("dp", "seq"), None),
            P(("dp", "seq"), "tensor"),
            P(("dp", "seq"), "tensor"),
            P(("dp", "seq")),
            P("tensor"),
        ),
        out_specs=(P("dp", "tensor"), P(("dp", "seq"), "tensor"), P(("dp", "seq")), P("tensor")),
        check_vma=False,
    )
```

```python
import jax
import jax.numpy as jnp
from jax import lax
from jax.experimental import pallas as pl
from jax.experimental.pallas import tpu as pltpu
from jax.sharding import PartitionSpec as P

D = 4096
FF_WIN = 7168
decay_rate = 0.8
learn_rate = 0.05
small_term = 1e-06

N = 4
NZ = 8
TOK = 512
ROWS = 224
COLS = 512
HALF = FF_WIN // 2
CHUNK = HALF // N
H = 128
G = 8
MSG = ROWS + G
POWER = 9.0
TOP = 15000.0
OFFS = (2, 1, 3, 0)
MESH = pl.DeviceIdType.MESH


def pick(i, values):
    out = values[-1]
    for n in range(len(values) - 2, -1, -1):
        out = jnp.where(i == n, values[n], out)
    return out


def encode(ref, value):
    groups = value.reshape(ROWS // G, G, H)
    peak = jnp.maximum(jnp.max(jnp.abs(groups), axis=0), 1e-30).astype(jnp.bfloat16)
    scale = TOP / peak.astype(jnp.float32)
    u = groups * scale[None]
    u2 = u * u
    u4 = u2 * u2
    u8 = u4 * u4
    ref[pl.ds(0, ROWS), :] = (u8 * u).astype(jnp.bfloat16).reshape(ROWS, H)
    ref[pl.ds(ROWS, G), :] = peak


def decode(ref):
    code = ref[pl.ds(0, ROWS), :].astype(jnp.float32).reshape(ROWS // G, G, H)
    scale = ref[pl.ds(ROWS, G), :].astype(jnp.float32) * (1.0 / TOP)
    size = jnp.exp(jnp.log(jnp.maximum(jnp.abs(code), 1.2e-38)) * (1.0 / POWER))
    return (size * jnp.where(code < 0.0, -scale[None], scale[None])).reshape(ROWS, H)


def kernel(
    hid, gout, master, rprev, cprev,
    nw, upd, nrow, ncol,
    h_own, h_par, g_own, g_par, flat, s1buf, r1buf, s2buf, r2buf, grad, mas, rp, cp,
    rowx, tall, plane, colc, sizx,
    ld_sem, xs_sem, xr_sem, s1s, r1s, s2s, r2s, zs, zr, cs, cr, ps, pr, ss, sr, ws, wr, bs, br, a2s, a2r, chain,
):
    c = lax.axis_index("dp")
    s = lax.axis_index("seq")
    z = lax.axis_index("tensor")
    x = s // N
    y = s % N

    def wrap(v):
        return lax.rem(v + N, N)

    def at(px, py):
        return (c, wrap(px) * N + wrap(py), z)

    partner = (1 - c, s, z)
    peers_plane = [at(x + d // N, y + d % N) for d in range(1, N * N)]
    peers_z = [(c, s, lax.rem(z + d, NZ)) for d in range(1, NZ)]
    right_x, left_x = at(x + 1, y), at(x - 1, y)
    right_y, left_y = at(x, y + 1), at(x, y - 1)
    link1 = [right_x, left_x, right_y, left_y]
    link2 = [right_y, left_y, right_x, left_x]
    near = link1 + [peers_z[0], peers_z[-1]]

    barrier = pltpu.get_barrier_semaphore()
    for peer in [partner] + near:
        pl.semaphore_signal(barrier, inc=1, device_id=peer, device_id_type=MESH)

    first = 1 - y // 2
    near_window = pl.ds(pl.multiple_of(first * 384, 128), 512)
    far_window = pl.ds(pl.multiple_of((1 - first) * 512, 128), 384)

    def start_of(core, j):
        return core * HALF + wrap(x + pick(j, OFFS)) * CHUNK

    def columns(core, j):
        return pl.ds(pl.multiple_of(start_of(core, j), 128), CHUNK)

    def load(src, dst, n):
        return pltpu.make_async_copy(src, dst, ld_sem.at[n])

    def load_h(j):
        return load(hid.at[:, columns(c, j)], h_own.at[j], j)

    load_g = load(gout, g_own, 4)
    small = [load(master, mas, 5), load(rprev, rp, 6), load(cprev, cp, 7)]
    load_g.start()
    for j in range(N):
        load_h(j).start()
    pl.semaphore_wait(barrier, 1 + len(near))

    def remote(src, dst, send, recv, peer):
        return pltpu.make_async_remote_copy(
            src_ref=src, dst_ref=dst, send_sem=send, recv_sem=recv, device_id=peer, device_id_type=MESH
        )

    def tell(n):
        for peer in near:
            pl.semaphore_signal(chain.at[n], inc=1, device_id=peer, device_id_type=MESH)

    def told(n):
        pl.semaphore_wait(chain.at[n], len(near))

    base = start_of(1 - c, 0)
    src_near = pl.ds(pl.multiple_of(base + first * 384, 128), 512)
    src_far = pl.ds(pl.multiple_of(base + (1 - first) * 512, 128), 384)

    def swap(n, src, dst):
        return remote(src, dst, xs_sem.at[n], xr_sem.at[n], partner)

    def swap_h(j):
        return swap(j, hid.at[:, columns(1 - c, j)], h_par.at[j])

    swap_near = swap(0, hid.at[:, src_near], h_par.at[0, :, near_window])
    swap_far = swap(6, hid.at[:, src_far], h_par.at[0, :, far_window])
    swap_g = swap(4, gout, g_par)
    swaps = [swap_g, swap_near, swap_far] + [swap_h(j) for j in range(1, N)]
    for copy in swaps:
        copy.start()
    for copy in small:
        copy.start()
    tell(0)

    def msg1(k, kind, i):
        return remote(s1buf.at[k, kind, i], r1buf.at[k, kind, i], s1s.at[k, kind, i], r1s.at[k, kind, i], link1[k])

    def msg2(k, kind):
        return remote(s2buf.at[k, kind], r2buf.at[k, kind], s2s.at[k, kind], r2s.at[k, kind], link2[k])

    def own(k):
        return pl.ds(k * H, H)

    def other(k):
        return pl.ds((k ^ 1) * H, H)

    def y_of(i):
        return pick(i, (wrap(y + 2), wrap(y + 2) + 1 - 2 * (y % 2), y + 1 - 2 * (y % 2), y))

    def part(j, v, cols):
        return flat.at[j, pl.ds(pl.multiple_of(v * ROWS, 32), ROWS), cols]

    def send1(k, kind, i, value):
        encode(s1buf.at[k, kind, i], value)
        msg1(k, kind, i).start()

    dims = (((0,), (0,)), ((), ()))

    def dot(h, g):
        return lax.dot_general(h, g, dims, preferred_element_type=jnp.float32)

    def ahead(k):
        return 1 if (k & 1) == 0 else -1

    def send_b1(j):
        for k in (2, 3):
            send1(k, 0, j, part(j, wrap(y + 2), own(k))[...])

    def send_b2(j):
        for k in (2, 3):
            send1(k, 1, j, part(j, wrap(y + ahead(k)), other(k))[...])

    def send_a(i, carry):
        for k in (0, 1):
            send1(k, 0, i, part(0, y_of(i), own(k))[...])
        return carry

    load_g.wait()
    load_h(0).wait()
    flat[0] = dot(h_own[0], g_own[...])
    swap_g.wait_recv()
    swap_near.wait_recv()
    flat[0, near_window, :] += dot(h_par[0, :, near_window], g_par[...])
    send_a(0, 0)
    send_b1(0)
    send_a(1, 0)
    swap_far.wait_recv()
    flat[0, far_window, :] += dot(h_par[0, :, far_window], g_par[...])
    lax.fori_loop(2, N, send_a, 0)
    send_b2(0)
    told(0)
    tell(1)

    def chunk(j, carry):
        load_h(j).wait()
        flat[j] = dot(h_own[j], g_own[...])
        swap_h(j).wait_recv()
        flat[j] += dot(h_par[j], g_par[...])
        send_b1(j)
        send_b2(j)

        for k in (0, 1):

            @pl.when(j == 1 + k)
            def _():
                def body(i, carry):
                    send1(k, 1, i, part(1 + k, y_of(i), other(k))[...])
                    return carry

                lax.fori_loop(0, N, body, 0)

        return carry

    lax.fori_loop(1, N, chunk, 0)
    told(1)
    tell(2)

    def target(k, i):
        if k < 2:
            return part(1 + k, y_of(i), own(k))
        return part(i, wrap(y + ahead(k)), own(k))

    def combine(i, carry):
        for k in range(4):
            msg1(k, 0, i).wait_recv()
            send1(k, 2, i, target(k, i)[...] + decode(r1buf.at[k, 0, i]))
        return carry

    lax.fori_loop(0, N, combine, 0)

    def mine(k, i):
        if k < 2:
            return part(3, y_of(i), own(k))
        return part(i, y, own(k))

    def beyond(k, cols):
        if k < 2:
            return part(3, wrap(y + ahead(k)), cols)
        return part(1 + (k & 1), y, cols)

    def send2(k, kind, value):
        encode(s2buf.at[k, kind], value)
        msg2(k, kind).start()

    def settle(i, carry):
        for k in range(4):
            msg1(k, 1, i).wait_recv()
            msg1(k, 2, i).wait_recv()
        for k in range(4):
            mine(k, i)[...] += decode(r1buf.at[k, 2, i]) + decode(r1buf.at[k ^ 1, 1, i])

        @pl.when(i == 0)
        def _():
            for k in range(4):
                send2(k, 0, mine(k, 0)[...])

        @pl.when(i == 2)
        def _():
            for k in range(4):
                send2(k, 1, beyond(k, other(k))[...])

        return carry

    lax.fori_loop(0, N - 1, settle, 0)
    for k in range(4):
        msg2(k, 0).wait_recv()
        send2(k, 2, beyond(k, own(k))[...] + decode(r2buf.at[k, 0]))
    settle(jnp.int32(3), 0)
    told(2)
    for k in range(4):
        msg2(k, 1).wait_recv()
    for k in range(4):
        msg2(k, 2).wait_recv()
    for k in range(4):
        grad[:, own(k)] = mine(k, 3)[...] + decode(r2buf.at[k, 2]) + decode(r2buf.at[k ^ 1, 1])

    g = grad[...]
    squares = g * g + small_term
    folded = squares[:, 0:128] + squares[:, 128:256] + squares[:, 256:384] + squares[:, 384:512]
    tall[pl.ds(0, ROWS), :] = folded
    tall[pl.ds(ROWS, 256 - ROWS), :] = jnp.zeros((256 - ROWS, 128), jnp.float32)
    rowx[z] = jnp.sum(tall[...].T, axis=0, keepdims=True)

    def exchange(ref, slot, peers, send, recv):
        copies = [remote(ref.at[slot], ref.at[slot], send.at[n], recv.at[n], peer) for n, peer in enumerate(peers)]
        for copy in copies:
            copy.start()
        return copies

    def arrive(copies):
        for copy in copies:
            copy.wait_recv()
        return copies

    pending = exchange(rowx, z, peers_z, zs, zr)
    col_sum = jnp.sum(squares, axis=0, keepdims=True)
    for copy in small:
        copy.wait()
    arrive(pending)
    row_total = jnp.sum(rowx[...], axis=0)
    new_rows = decay_rate * rp[...] + (1.0 - decay_rate) * row_total[:, 0:ROWS] / D
    nrow[...] = new_rows
    wide = jnp.concatenate([new_rows, jnp.ones((1, 256 - ROWS), jnp.float32)], axis=1)
    row_scale = jnp.broadcast_to(lax.rsqrt(wide), (128, 256)).T[0:ROWS, :]
    scaled = g * jnp.concatenate([row_scale] * 4, axis=1)

    colc[c, pl.ds(0, 1), :] = col_sum
    colc[c, pl.ds(1, 1), :] = jnp.sum(scaled * scaled, axis=0, keepdims=True)
    pending += arrive(exchange(colc, c, [partner], cs, cr))
    plane[s] = colc[0] + colc[1]
    pending += arrive(exchange(plane, s, peers_plane, ps, pr))
    both = jnp.sum(plane[...], axis=0)
    new_cols = decay_rate * cp[...] + (1.0 - decay_rate) * both[0:1] / FF_WIN
    ncol[...] = new_cols
    ratio = both[1:2] / new_cols
    short = ratio[:, 0:128] + ratio[:, 128:256] + ratio[:, 256:384] + ratio[:, 384:512]
    sizx[z] = short
    last = exchange(sizx, z, peers_z, ss, sr)
    raw = scaled * lax.rsqrt(new_cols)
    pending += arrive(last)
    raw_total = jnp.sum(jnp.sum(sizx[...], axis=0), axis=1, keepdims=True)
    size = jnp.sqrt(raw_total / (FF_WIN * D))
    update = raw * (1.0 / jnp.maximum(1.0, size))
    nw[s] = (mas[...] - learn_rate * update).astype(jnp.bfloat16)

    def block(px, py):
        return wrap(px) * N + wrap(py)

    def pair(k):
        return pl.ds((k // 2) * 2 * H, 2 * H)

    def gather(send, recv, src, cols, peer):
        return remote(nw.at[src, :, cols], nw.at[src, :, cols], send, recv, peer)

    from_link = [block(x - 1, y), block(x + 1, y), block(x, y - 1), block(x, y + 1)]
    opposite = [block(x + 2, y), block(x, y + 2)]

    def direct(k, part_of, src):
        return gather(ws.at[k, part_of], wr.at[k, part_of], src, pl.ds(part_of * 2 * H, 2 * H), link1[k])

    def relay(k, src):
        return gather(bs.at[k], br.at[k], src, pl.ds((k & 1) * 2 * H, 2 * H), link1[k])

    def second(k, n, src):
        return gather(a2s.at[k, n, 0], a2r.at[k, n, 0], src, pair(k), link2[k])

    def beside(k, n):
        step = (-1, 1, 2)[n]
        return block(x + step, y - ahead(k)) if k < 2 else block(x - ahead(k), y + step)

    def third(k, n):
        return gather(a2s.at[k, n, 1], a2r.at[k, n, 1], beside(k, n), own(k), link2[k])

    sends = []

    def go(copy):
        copy.start()
        sends.append(copy)

    for k in range(4):
        go(direct(k, k // 2, s))
    for k in range(4):
        go(direct(k, 1 - k // 2, s))
    upd[...] = update
    for k in (0, 3, 1, 2):
        direct(k, k // 2, from_link[k]).wait_recv()
        if k in (0, 3):
            go(relay(k, from_link[k]))
        for side in (0, 1):
            go(second((k & 2) + side, k & 1, from_link[k]))
    for k in (1, 2):
        direct(k, 1 - k // 2, from_link[k]).wait_recv()
        go(relay(k, from_link[k]))
    for k, axis in ((0, 0), (3, 1)):
        relay(k, opposite[axis]).wait_recv()
        for side in (0, 1):
            go(second(axis * 2 + side, 2, opposite[axis]))
    for n in range(3):
        for k in range(4):
            second(k, n, beside(k, n)).wait_recv()
            go(third(k, n))
    for k in (0, 3):
        direct(k, 1 - k // 2, from_link[k]).wait_recv()
    relay(1, opposite[0]).wait_recv()
    relay(2, opposite[1]).wait_recv()
    for n in range(3):
        for k in range(4):
            third(k, n).wait_recv()

    for copy in sends + pending + swaps:
        copy.wait_send()

    def drain(i, carry):
        for k in range(4):
            for kind in range(3):
                msg1(k, kind, i).wait_send()
        return carry

    lax.fori_loop(0, N, drain, 0)
    for k in range(4):
        for kind in range(3):
            msg2(k, kind).wait_send()


def writer(nw, upd, nrow, ncol, nw_out, upd_out, nrow_out, ncol_out, sem):
    quarter = N * N // 4
    pairs = [(nw.at[pl.ds(n * quarter, quarter)], nw_out.at[pl.ds(n * quarter, quarter)]) for n in range(4)]
    pairs += [(upd, upd_out), (nrow, nrow_out), (ncol, ncol_out)]
    copies = [pltpu.make_async_copy(src, dst, sem.at[n]) for n, (src, dst) in enumerate(pairs)]
    for copy in copies:
        copy.start()
    for copy in copies:
        copy.wait()


def per_device(hidden, grad_out, master_weight, row_prev, col_prev):
    hbm = pl.BlockSpec(memory_space=pltpu.HBM)
    vmem = pl.BlockSpec(memory_space=pltpu.VMEM)
    f32, bf16 = jnp.float32, jnp.bfloat16
    dma = pltpu.SemaphoreType.DMA
    results = (((N * N, ROWS, COLS), bf16), ((ROWS, COLS), f32), ((1, ROWS), f32), ((1, COLS), f32))
    held = pl.pallas_call(
        kernel,
        out_shape=tuple(pltpu.VMEM(shape, kind) for shape, kind in results),
        in_specs=[hbm] * 5,
        out_specs=(vmem,) * 4,
        scratch_shapes=[
            pltpu.VMEM((N, TOK, CHUNK), bf16),
            pltpu.VMEM((N, TOK, CHUNK), bf16),
            pltpu.VMEM((TOK, COLS), bf16),
            pltpu.VMEM((TOK, COLS), bf16),
            pltpu.VMEM((N, CHUNK, COLS), f32),
            pltpu.VMEM((4, 3, N, MSG, H), bf16),
            pltpu.VMEM((4, 3, N, MSG, H), bf16),
            pltpu.VMEM((4, 3, MSG, H), bf16),
            pltpu.VMEM((4, 3, MSG, H), bf16),
            pltpu.VMEM((ROWS, COLS), f32),
            pltpu.VMEM((ROWS, COLS), f32),
            pltpu.VMEM((1, ROWS), f32),
            pltpu.VMEM((1, COLS), f32),
            pltpu.VMEM((NZ, 1, 256), f32),
            pltpu.VMEM((256, 128), f32),
            pltpu.VMEM((N * N, 2, COLS), f32),
            pltpu.VMEM((2, 2, COLS), f32),
            pltpu.VMEM((NZ, 1, 128), f32),
            dma((8,)), dma((7,)), dma((7,)),
            dma((4, 3, N)), dma((4, 3, N)), dma((4, 3)), dma((4, 3)),
            dma((NZ - 1,)), dma((NZ - 1,)), dma((1,)), dma((1,)), dma((N * N - 1,)), dma((N * N - 1,)),
            dma((NZ - 1,)), dma((NZ - 1,)),
            dma((4, 2)), dma((4, 2)), dma((4,)), dma((4,)), dma((4, 3, 2)), dma((4, 3, 2)),
            pltpu.SemaphoreType.REGULAR((3,)),
        ],
        compiler_params=pltpu.CompilerParams(collective_id=0, has_side_effects=True, vmem_limit_bytes=62700000),
    )(hidden, grad_out, master_weight, row_prev.reshape(1, ROWS), col_prev.reshape(1, COLS))
    nw, upd, nrows, ncols = pl.pallas_call(
        writer,
        out_shape=tuple(jax.ShapeDtypeStruct(shape, kind) for shape, kind in results),
        in_specs=[vmem] * 4,
        out_specs=(hbm,) * 4,
        scratch_shapes=[dma((7,))],
        compiler_params=pltpu.CompilerParams(vmem_limit_bytes=1024 * 1024),
    )(*held)
    return nw.reshape(HALF, COLS), upd, nrows.reshape(ROWS), ncols.reshape(COLS)


def solution(mesh):
    return jax.shard_map(
        per_device,
        mesh=mesh,
        in_specs=(
            P(("dp", "seq"), None),
            P(("dp", "seq"), "tensor"),
            P(("dp", "seq"), "tensor"),
            P(("dp", "seq")),
            P("tensor"),
        ),
        out_specs=(P("dp", "tensor"), P(("dp", "seq"), "tensor"), P(("dp", "seq")), P("tensor")),
        check_vma=False,
    )
```

```python
import jax
import jax.numpy as jnp
from jax import lax
from jax.experimental import pallas as pl
from jax.experimental.pallas import tpu as pltpu
from jax.sharding import PartitionSpec as P

D = 4096
FF_WIN = 7168
decay_rate = 0.8
learn_rate = 0.05
small_term = 1e-06

N = 4
NZ = 8
TOK = 512
ROWS = 224
COLS = 512
HALF = FF_WIN // 2
CHUNK = HALF // N
H = 128
G = 8
MSG = ROWS + G
POWER = 9.0
TOP = 15000.0
OFFS = (2, 1, 3, 0)
MESH = pl.DeviceIdType.MESH


def pick(i, values):
    out = values[-1]
    for n in range(len(values) - 2, -1, -1):
        out = jnp.where(i == n, values[n], out)
    return out


def encode(ref, value):
    groups = value.reshape(ROWS // G, G, value.shape[1])
    peak = jnp.maximum(jnp.max(jnp.abs(groups), axis=0), 1e-30).astype(jnp.bfloat16)
    scale = TOP / peak.astype(jnp.float32)
    u = groups * scale[None]
    u2 = u * u
    u4 = u2 * u2
    u8 = u4 * u4
    ref[pl.ds(0, ROWS), :] = (u8 * u).astype(jnp.bfloat16).reshape(value.shape)
    ref[pl.ds(ROWS, G), :] = peak


def decode(ref):
    width = ref.shape[1]
    code = ref[pl.ds(0, ROWS), :].astype(jnp.float32).reshape(ROWS // G, G, width)
    scale = ref[pl.ds(ROWS, G), :].astype(jnp.float32) * (1.0 / TOP)
    size = jnp.exp(jnp.log(jnp.maximum(jnp.abs(code), 1.2e-38)) * (1.0 / POWER))
    return (size * jnp.where(code < 0.0, -scale[None], scale[None])).reshape(ROWS, width)


def kernel(
    hid, gout, master, rprev, cprev,
    nw, upd, nrow, ncol,
    h_own, h_par, g_own, g_par, flat, s1buf, r1buf, s2buf, r2buf, grad, mas, rp, cp,
    rowx, tall, plane, colc, sizx, mnear, rcode, rnear, dnear, down,
    ld_sem, xs_sem, xr_sem, s1s, r1s, s2s, r2s, zs, zr, cs, cr, ps, pr, ss, sr, ws, wr, bs, br, a2s, a2r, es, er, fs, fr, chain,
):
    c = lax.axis_index("dp")
    s = lax.axis_index("seq")
    z = lax.axis_index("tensor")
    x = s // N
    y = s % N

    def wrap(v):
        return lax.rem(v + N, N)

    def at(px, py):
        return (c, wrap(px) * N + wrap(py), z)

    partner = (1 - c, s, z)
    peers_plane = [at(x + d // N, y + d % N) for d in range(1, N * N)]
    peers_z = [(c, s, lax.rem(z + d, NZ)) for d in range(1, NZ)]
    right_x, left_x = at(x + 1, y), at(x - 1, y)
    right_y, left_y = at(x, y + 1), at(x, y - 1)
    link1 = [right_x, left_x, right_y, left_y]
    link2 = [right_y, left_y, right_x, left_x]
    near = link1 + [peers_z[0], peers_z[-1]]

    barrier = pltpu.get_barrier_semaphore()
    for peer in [partner] + near:
        pl.semaphore_signal(barrier, inc=1, device_id=peer, device_id_type=MESH)

    first = 1 - y // 2
    near_window = pl.ds(pl.multiple_of(first * 384, 128), 512)
    far_window = pl.ds(pl.multiple_of((1 - first) * 512, 128), 384)

    def start_of(core, j):
        return core * HALF + wrap(x + pick(j, OFFS)) * CHUNK

    def columns(core, j):
        return pl.ds(pl.multiple_of(start_of(core, j), 128), CHUNK)

    def load(src, dst, n):
        return pltpu.make_async_copy(src, dst, ld_sem.at[n])

    def load_h(j):
        return load(hid.at[:, columns(c, j)], h_own.at[j], j)

    load_g = load(gout, g_own, 4)
    small = [load(master, mas, 5), load(rprev, rp, 6), load(cprev, cp, 7)]
    load_g.start()
    for j in range(N):
        load_h(j).start()
    pl.semaphore_wait(barrier, 1 + len(near))

    def remote(src, dst, send, recv, peer):
        return pltpu.make_async_remote_copy(
            src_ref=src, dst_ref=dst, send_sem=send, recv_sem=recv, device_id=peer, device_id_type=MESH
        )

    def tell(n):
        for peer in near:
            pl.semaphore_signal(chain.at[n], inc=1, device_id=peer, device_id_type=MESH)

    def told(n):
        pl.semaphore_wait(chain.at[n], len(near))

    base = start_of(1 - c, 0)
    src_near = pl.ds(pl.multiple_of(base + first * 384, 128), 512)
    src_far = pl.ds(pl.multiple_of(base + (1 - first) * 512, 128), 384)

    def swap(n, src, dst):
        return remote(src, dst, xs_sem.at[n], xr_sem.at[n], partner)

    def swap_h(j):
        return swap(j, hid.at[:, columns(1 - c, j)], h_par.at[j])

    swap_near = swap(0, hid.at[:, src_near], h_par.at[0, :, near_window])
    swap_far = swap(6, hid.at[:, src_far], h_par.at[0, :, far_window])
    swap_g = swap(4, gout, g_par)
    swaps = [swap_g, swap_near, swap_far] + [swap_h(j) for j in range(1, N)]
    for copy in swaps:
        copy.start()
    for copy in small:
        copy.start()

    def early(k, turn):
        rows = pl.ds(turn * (ROWS // 2), ROWS // 2)
        lanes = pl.ds((k // 2) * 2 * H, 2 * H)
        return remote(master.at[rows, lanes], mnear.at[k, rows], es.at[k, turn], er.at[k, turn], link1[k])

    tell(0)

    def way(i):
        return 1 - 2 * (i % 2)

    def cols(axis):
        return pl.ds(axis * 2 * H, 2 * H)

    def msg1(axis, kind, i):
        step = -way(i) if kind == 1 else way(i)
        peer = at(x + step, y) if axis == 0 else at(x, y + step)
        index = (axis, kind, i)
        return remote(s1buf.at[index], r1buf.at[index], s1s.at[index], r1s.at[index], peer)

    def msg2(k, kind):
        return remote(s2buf.at[k, kind], r2buf.at[k, kind], s2s.at[k, kind], r2s.at[k, kind], link2[k])

    def own(k):
        return pl.ds(k * H, H)

    def other(k):
        return pl.ds((k ^ 1) * H, H)

    def y_of(i):
        return pick(i, (wrap(y + 2), wrap(y + 2) + 1 - 2 * (y % 2), y + 1 - 2 * (y % 2), y))

    def part(j, v, cols):
        return flat.at[j, pl.ds(pl.multiple_of(v * ROWS, 32), ROWS), cols]

    def send1(axis, kind, i, value):
        encode(s1buf.at[axis, kind, i], value)
        msg1(axis, kind, i).start()

    dims = (((0,), (0,)), ((), ()))

    def dot(h, g):
        return lax.dot_general(h, g, dims, preferred_element_type=jnp.float32)

    def ahead(k):
        return 1 if (k & 1) == 0 else -1

    def send_b1(j):
        send1(1, 0, j, part(j, wrap(y + 2), cols(1))[...])

    def send_b2(j):
        send1(1, 1, j, part(j, wrap(y - way(j)), cols(1))[...])

    def send_a(i, carry):
        send1(0, 0, i, part(0, y_of(i), cols(0))[...])
        return carry

    load_g.wait()
    load_h(0).wait()
    flat[0] = dot(h_own[0], g_own[...])
    swap_g.wait_recv()
    swap_near.wait_recv()
    flat[0, near_window, :] += dot(h_par[0, :, near_window], g_par[...])
    send_a(0, 0)
    send_b1(0)
    send_a(1, 0)
    swap_far.wait_recv()
    flat[0, far_window, :] += dot(h_par[0, :, far_window], g_par[...])
    lax.fori_loop(2, N, send_a, 0)
    send_b2(0)
    told(0)
    tell(1)

    def chunk(j, carry):
        load_h(j).wait()
        flat[j] = dot(h_own[j], g_own[...])
        swap_h(j).wait_recv()
        flat[j] += dot(h_par[j], g_par[...])
        send_b1(j)
        send_b2(j)

        @pl.when(j < 3)
        def _():
            def body(m, carry):
                i = 2 * m + 2 - j
                send1(0, 1, i, part(j, y_of(i), cols(0))[...])
                return carry

            lax.fori_loop(0, 2, body, 0)

        return carry

    lax.fori_loop(1, N, chunk, 0)
    told(1)
    tell(2)

    def combine(i, carry):
        for axis in (0, 1):
            msg1(axis, 0, i).wait_recv()
            mid = part(1 + i % 2, y_of(i), cols(0)) if axis == 0 else part(i, wrap(y + way(i)), cols(1))
            send1(axis, 2, i, mid[...] + decode(r1buf.at[axis, 0, i]))
        return carry

    lax.fori_loop(0, N, combine, 0)

    def mine(k, i):
        return part(3, y_of(i), own(k)) if k < 2 else part(i, y, own(k))

    def beyond(k, lanes):
        if k < 2:
            return part(3, wrap(y + ahead(k)), lanes)
        return part(1 + (k & 1), y, lanes)

    def send2(k, kind, value):
        encode(s2buf.at[k, kind], value)
        msg2(k, kind).start()

    def settle(i, carry):
        for axis in (0, 1):
            msg1(axis, 1, i).wait_recv()
            msg1(axis, 2, i).wait_recv()
            ref = part(3, y_of(i), cols(0)) if axis == 0 else part(i, y, cols(1))
            ref[...] += decode(r1buf.at[axis, 1, i]) + decode(r1buf.at[axis, 2, i])

        @pl.when(i == 0)
        def _():
            for k in range(4):
                send2(k, 0, mine(k, 0)[...])

        @pl.when(i == 2)
        def _():
            for k in range(4):
                send2(k, 1, beyond(k, other(k))[...])

        return carry

    lax.fori_loop(0, N - 1, settle, 0)
    for k in range(4):
        msg2(k, 0).wait_recv()
        send2(k, 2, beyond(k, own(k))[...] + decode(r2buf.at[k, 0]))
    settle(jnp.int32(3), 0)
    told(2)
    for k in range(4):
        msg2(k, 1).wait_recv()
    for k in range(4):
        grad[:, own(k)] = mine(k, 3)[...] + decode(r2buf.at[k ^ 1, 1])
    folded = jnp.zeros((ROWS, H), jnp.float32)
    for k in range(4):
        msg2(k, 2).wait_recv()
        final = grad[:, own(k)] + decode(r2buf.at[k, 2])
        grad[:, own(k)] = final
        folded = folded + (final * final + small_term)

    tall[pl.ds(0, ROWS), :] = folded
    tall[pl.ds(ROWS, 256 - ROWS), :] = jnp.zeros((256 - ROWS, 128), jnp.float32)
    rowx[z] = jnp.sum(tall[...].T, axis=0, keepdims=True)

    def exchange(ref, slot, peers, send, recv):
        copies = [remote(ref.at[slot], ref.at[slot], send.at[n], recv.at[n], peer) for n, peer in enumerate(peers)]
        for copy in copies:
            copy.start()
        return copies

    def arrive(copies):
        for copy in copies:
            copy.wait_recv()
        return copies

    pending = exchange(rowx, z, peers_z, zs, zr)
    for turn in (0, 1):
        for k in range(4):
            early(k, turn).start()
    g = grad[...]
    col_sum = jnp.sum(g * g + small_term, axis=0, keepdims=True)
    for copy in small:
        copy.wait()
    arrive(pending)
    row_total = jnp.sum(rowx[...], axis=0)
    new_rows = decay_rate * rp[...] + (1.0 - decay_rate) * row_total[:, 0:ROWS] / D
    nrow[...] = new_rows
    wide = jnp.concatenate([new_rows, jnp.ones((1, 256 - ROWS), jnp.float32)], axis=1)
    row_scale = jnp.broadcast_to(lax.rsqrt(wide), (128, 256)).T[0:ROWS, :]
    scaled = g * jnp.concatenate([row_scale] * 4, axis=1)

    colc[c, pl.ds(0, 1), :] = col_sum
    colc[c, pl.ds(1, 1), :] = jnp.sum(scaled * scaled, axis=0, keepdims=True)
    pending += arrive(exchange(colc, c, [partner], cs, cr))
    plane[s] = colc[0] + colc[1]
    pending += arrive(exchange(plane, s, peers_plane, ps, pr))
    both = jnp.sum(plane[...], axis=0)
    new_cols = decay_rate * cp[...] + (1.0 - decay_rate) * both[0:1] / FF_WIN
    ncol[...] = new_cols
    ratio = both[1:2] / new_cols
    short = ratio[:, 0:128] + ratio[:, 128:256] + ratio[:, 256:384] + ratio[:, 384:512]
    sizx[z] = short
    last = exchange(sizx, z, peers_z, ss, sr)
    raw = scaled * lax.rsqrt(new_cols)

    def code(k):
        return remote(rcode.at[k // 2], rnear.at[k], fs.at[k], fr.at[k], link1[k])

    for axis in (0, 1):
        encode(rcode.at[axis], raw[:, axis * 2 * H : (axis + 1) * 2 * H])
        for k in (2 * axis, 2 * axis + 1):
            code(k).start()
    for axis in (0, 1):
        down[:, cols(axis)] = decode(rcode.at[axis])
    for k in (0, 2, 1, 3):
        code(k).wait_recv()
        dnear[k] = decode(rnear.at[k])
        early(k, 0).wait_recv()
        early(k, 1).wait_recv()
    pending += arrive(last)
    raw_total = jnp.sum(jnp.sum(sizx[...], axis=0), axis=1, keepdims=True)
    size = jnp.sqrt(raw_total / (FF_WIN * D))
    clip = 1.0 / jnp.maximum(1.0, size)

    def fresh(weight, step):
        return (weight - learn_rate * (step * clip)).astype(jnp.bfloat16)

    nw[s] = fresh(mas[...], down[...])

    def block(px, py):
        return wrap(px) * N + wrap(py)

    def pair(k):
        return pl.ds((k // 2) * 2 * H, 2 * H)

    def gather(send, recv, src, cols, peer):
        return remote(nw.at[src, :, cols], nw.at[src, :, cols], send, recv, peer)

    from_link = [block(x - 1, y), block(x + 1, y), block(x, y - 1), block(x, y + 1)]
    opposite = [block(x + 2, y), block(x, y + 2)]

    def direct(k, part_of, src):
        return gather(ws.at[k, part_of], wr.at[k, part_of], src, pl.ds(part_of * 2 * H, 2 * H), link1[k])

    def relay(k, src):
        return gather(bs.at[k], br.at[k], src, pl.ds((k & 1) * 2 * H, 2 * H), link1[k])

    def second(k, n, src):
        return gather(a2s.at[k, n, 0], a2r.at[k, n, 0], src, pair(k), link2[k])

    def beside(k, n):
        step = (-1, 1, 2)[n]
        return block(x + step, y - ahead(k)) if k < 2 else block(x - ahead(k), y + step)

    def third(k, n):
        return gather(a2s.at[k, n, 1], a2r.at[k, n, 1], beside(k, n), own(k), link2[k])

    sends = []

    def go(copy):
        copy.start()
        sends.append(copy)

    for k in (1, 2, 0, 3):
        go(direct(k, 1 - k // 2, s))
    for k in (0, 3, 1, 2):
        nw[from_link[k], :, pair(k)] = fresh(mnear[k], dnear[k])
        if k in (0, 3):
            go(relay(k, from_link[k]))
        for side in (0, 1):
            go(second((k & 2) + side, k & 1, from_link[k]))
    upd[...] = raw * clip
    for k in (1, 2):
        direct(k, 1 - k // 2, from_link[k]).wait_recv()
        go(relay(k, from_link[k]))
    for k, axis in ((0, 0), (3, 1)):
        relay(k, opposite[axis]).wait_recv()
        for side in (0, 1):
            go(second(axis * 2 + side, 2, opposite[axis]))
    for n in range(3):
        for k in range(4):
            second(k, n, beside(k, n)).wait_recv()
            go(third(k, n))
    for k in (0, 3):
        direct(k, 1 - k // 2, from_link[k]).wait_recv()
    relay(1, opposite[0]).wait_recv()
    relay(2, opposite[1]).wait_recv()
    for n in range(3):
        for k in range(4):
            third(k, n).wait_recv()

    for copy in sends + pending + swaps:
        copy.wait_send()
    for k in range(4):
        early(k, 0).wait_send()
        early(k, 1).wait_send()
        code(k).wait_send()

    def drain(i, carry):
        for axis in (0, 1):
            for kind in range(3):
                msg1(axis, kind, i).wait_send()
        return carry

    lax.fori_loop(0, N, drain, 0)
    for k in range(4):
        for kind in range(3):
            msg2(k, kind).wait_send()


def writer(nw, upd, nrow, ncol, nw_out, upd_out, nrow_out, ncol_out, sem):
    quarter = N * N // 4
    pairs = [(nw.at[pl.ds(n * quarter, quarter)], nw_out.at[pl.ds(n * quarter, quarter)]) for n in range(4)]
    pairs += [(upd, upd_out), (nrow, nrow_out), (ncol, ncol_out)]
    copies = [pltpu.make_async_copy(src, dst, sem.at[n]) for n, (src, dst) in enumerate(pairs)]
    for copy in copies:
        copy.start()
    for copy in copies:
        copy.wait()


def per_device(hidden, grad_out, master_weight, row_prev, col_prev):
    hbm = pl.BlockSpec(memory_space=pltpu.HBM)
    vmem = pl.BlockSpec(memory_space=pltpu.VMEM)
    f32, bf16 = jnp.float32, jnp.bfloat16
    dma = pltpu.SemaphoreType.DMA
    results = (((N * N, ROWS, COLS), bf16), ((ROWS, COLS), f32), ((1, ROWS), f32), ((1, COLS), f32))
    held = pl.pallas_call(
        kernel,
        out_shape=tuple(pltpu.VMEM(shape, kind) for shape, kind in results),
        in_specs=[hbm] * 5,
        out_specs=(vmem,) * 4,
        scratch_shapes=[
            pltpu.VMEM((N, TOK, CHUNK), bf16),
            pltpu.VMEM((N, TOK, CHUNK), bf16),
            pltpu.VMEM((TOK, COLS), bf16),
            pltpu.VMEM((TOK, COLS), bf16),
            pltpu.VMEM((N, CHUNK, COLS), f32),
            pltpu.VMEM((2, 3, N, MSG, 2 * H), bf16),
            pltpu.VMEM((2, 3, N, MSG, 2 * H), bf16),
            pltpu.VMEM((4, 3, MSG, H), bf16),
            pltpu.VMEM((4, 3, MSG, H), bf16),
            pltpu.VMEM((ROWS, COLS), f32),
            pltpu.VMEM((ROWS, COLS), f32),
            pltpu.VMEM((1, ROWS), f32),
            pltpu.VMEM((1, COLS), f32),
            pltpu.VMEM((NZ, 1, 256), f32),
            pltpu.VMEM((256, 128), f32),
            pltpu.VMEM((N * N, 2, COLS), f32),
            pltpu.VMEM((2, 2, COLS), f32),
            pltpu.VMEM((NZ, 1, 128), f32),
            pltpu.VMEM((4, ROWS, 2 * H), f32),
            pltpu.VMEM((2, MSG, 2 * H), bf16),
            pltpu.VMEM((4, MSG, 2 * H), bf16),
            pltpu.VMEM((4, ROWS, 2 * H), f32),
            pltpu.VMEM((ROWS, COLS), f32),
            dma((8,)), dma((7,)), dma((7,)),
            dma((2, 3, N)), dma((2, 3, N)), dma((4, 3)), dma((4, 3)),
            dma((NZ - 1,)), dma((NZ - 1,)), dma((1,)), dma((1,)), dma((N * N - 1,)), dma((N * N - 1,)),
            dma((NZ - 1,)), dma((NZ - 1,)),
            dma((4, 2)), dma((4, 2)), dma((4,)), dma((4,)), dma((4, 3, 2)), dma((4, 3, 2)),
            dma((4, 2)), dma((4, 2)), dma((4,)), dma((4,)),
            pltpu.SemaphoreType.REGULAR((3,)),
        ],
        compiler_params=pltpu.CompilerParams(collective_id=0, has_side_effects=True, vmem_limit_bytes=62700000),
    )(hidden, grad_out, master_weight, row_prev.reshape(1, ROWS), col_prev.reshape(1, COLS))
    nw, upd, nrows, ncols = pl.pallas_call(
        writer,
        out_shape=tuple(jax.ShapeDtypeStruct(shape, kind) for shape, kind in results),
        in_specs=[vmem] * 4,
        out_specs=(hbm,) * 4,
        scratch_shapes=[dma((7,))],
        compiler_params=pltpu.CompilerParams(vmem_limit_bytes=1024 * 1024),
    )(*held)
    return nw.reshape(HALF, COLS), upd, nrows.reshape(ROWS), ncols.reshape(COLS)


def solution(mesh):
    return jax.shard_map(
        per_device,
        mesh=mesh,
        in_specs=(
            P(("dp", "seq"), None),
            P(("dp", "seq"), "tensor"),
            P(("dp", "seq"), "tensor"),
            P(("dp", "seq")),
            P("tensor"),
        ),
        out_specs=(P("dp", "tensor"), P(("dp", "seq"), "tensor"), P(("dp", "seq")), P("tensor")),
        check_vma=False,
    )
```

```python
import jax
import jax.numpy as jnp
from jax import lax
from jax.experimental import pallas as pl
from jax.experimental.pallas import tpu as pltpu
from jax.sharding import PartitionSpec as P

D = 4096
FF_WIN = 7168
decay_rate = 0.8
learn_rate = 0.05
small_term = 1e-06

N = 4
NZ = 8
TOK = 512
ROWS = 224
COLS = 512
HALF = FF_WIN // 2
CHUNK = HALF // N
H = 128
G = 8
MSG = ROWS + G
POWER = 9.0
TOP = 15000.0
OFFS = (2, 1, 3, 0)
MESH = pl.DeviceIdType.MESH


def pick(i, values):
    out = values[-1]
    for n in range(len(values) - 2, -1, -1):
        out = jnp.where(i == n, values[n], out)
    return out


def encode(ref, value):
    groups = value.reshape(ROWS // G, G, value.shape[1])
    peak = jnp.maximum(jnp.max(jnp.abs(groups), axis=0), 1e-30).astype(jnp.bfloat16)
    scale = TOP / peak.astype(jnp.float32)
    u = groups * scale[None]
    u2 = u * u
    u4 = u2 * u2
    u8 = u4 * u4
    ref[pl.ds(0, ROWS), :] = (u8 * u).astype(jnp.bfloat16).reshape(value.shape)
    ref[pl.ds(ROWS, G), :] = peak


def decode(ref):
    width = ref.shape[1]
    code = ref[pl.ds(0, ROWS), :].astype(jnp.float32).reshape(ROWS // G, G, width)
    scale = ref[pl.ds(ROWS, G), :].astype(jnp.float32) * (1.0 / TOP)
    size = jnp.exp(jnp.log(jnp.maximum(jnp.abs(code), 1.2e-38)) * (1.0 / POWER))
    return (size * jnp.where(code < 0.0, -scale[None], scale[None])).reshape(ROWS, width)


def kernel(
    hid, gout, master, rprev, cprev,
    nw, upd, nrow, ncol,
    h_own, h_par, g_own, g_par, flat, s1buf, r1buf, s2buf, r2buf, grad, mas, rp, cp,
    rowx, tall, plane, colc, sizx, mnear, rcode, rnear, dnear, down,
    ld_sem, xs_sem, xr_sem, s1s, r1s, s2s, r2s, zs, zr, cs, cr, ps, pr, ss, sr, ws, wr, bs, br, a2s, a2r, es, er, fs, fr, chain,
):
    c = lax.axis_index("dp")
    s = lax.axis_index("seq")
    z = lax.axis_index("tensor")
    x = s // N
    y = s % N

    def wrap(v):
        return lax.rem(v + N, N)

    def at(px, py):
        return (c, wrap(px) * N + wrap(py), z)

    partner = (1 - c, s, z)
    peers_plane = [at(x + d // N, y + d % N) for d in range(1, N * N)]
    peers_z = [(c, s, lax.rem(z + d, NZ)) for d in range(1, NZ)]
    right_x, left_x = at(x + 1, y), at(x - 1, y)
    right_y, left_y = at(x, y + 1), at(x, y - 1)
    link1 = [right_x, left_x, right_y, left_y]
    link2 = [right_y, left_y, right_x, left_x]
    near = link1 + [peers_z[0], peers_z[-1]]

    barrier = pltpu.get_barrier_semaphore()
    for peer in [partner] + near:
        pl.semaphore_signal(barrier, inc=1, device_id=peer, device_id_type=MESH)

    first = 1 - y // 2
    near_window = pl.ds(pl.multiple_of(first * 384, 128), 512)
    far_window = pl.ds(pl.multiple_of((1 - first) * 512, 128), 384)

    def start_of(core, j):
        return core * HALF + wrap(x + pick(j, OFFS)) * CHUNK

    def columns(core, j):
        return pl.ds(pl.multiple_of(start_of(core, j), 128), CHUNK)

    def load(src, dst, n):
        return pltpu.make_async_copy(src, dst, ld_sem.at[n])

    def load_h(j):
        return load(hid.at[:, columns(c, j)], h_own.at[j], j)

    load_g = load(gout, g_own, 4)
    small = [load(master, mas, 5), load(rprev, rp, 6), load(cprev, cp, 7)]
    load_g.start()
    for j in range(N):
        load_h(j).start()
    pl.semaphore_wait(barrier, 1 + len(near))

    def remote(src, dst, send, recv, peer):
        return pltpu.make_async_remote_copy(
            src_ref=src, dst_ref=dst, send_sem=send, recv_sem=recv, device_id=peer, device_id_type=MESH
        )

    def tell(n):
        for peer in near:
            pl.semaphore_signal(chain.at[n], inc=1, device_id=peer, device_id_type=MESH)

    def told(n):
        pl.semaphore_wait(chain.at[n], len(near))

    base = start_of(1 - c, 0)
    src_near = pl.ds(pl.multiple_of(base + first * 384, 128), 512)
    src_far = pl.ds(pl.multiple_of(base + (1 - first) * 512, 128), 384)

    def swap(n, src, dst):
        return remote(src, dst, xs_sem.at[n], xr_sem.at[n], partner)

    def swap_h(j):
        return swap(j, hid.at[:, columns(1 - c, j)], h_par.at[j])

    swap_near = swap(0, hid.at[:, src_near], h_par.at[0, :, near_window])
    swap_far = swap(6, hid.at[:, src_far], h_par.at[0, :, far_window])
    swap_g = swap(4, gout, g_par)
    swaps = [swap_g, swap_near, swap_far] + [swap_h(j) for j in range(1, N)]
    for copy in swaps:
        copy.start()
    for copy in small:
        copy.start()

    def early(k, turn):
        rows = pl.ds(turn * (ROWS // 2), ROWS // 2)
        lanes = pl.ds((k // 2) * 2 * H, 2 * H)
        return remote(master.at[rows, lanes], mnear.at[k, rows], es.at[k, turn], er.at[k, turn], link1[k])

    tell(0)

    def way(i):
        return 1 - 2 * (i % 2)

    def cols(axis):
        return pl.ds(axis * 2 * H, 2 * H)

    def msg1(axis, kind, i):
        step = -way(i) if kind == 1 else way(i)
        peer = at(x + step, y) if axis == 0 else at(x, y + step)
        index = (axis, kind, i)
        return remote(s1buf.at[index], r1buf.at[index], s1s.at[index], r1s.at[index], peer)

    def msg2(k, kind):
        return remote(s2buf.at[k, kind], r2buf.at[k, kind], s2s.at[k, kind], r2s.at[k, kind], link2[k])

    def own(k):
        return pl.ds(k * H, H)

    def other(k):
        return pl.ds((k ^ 1) * H, H)

    def y_of(i):
        return pick(i, (wrap(y + 2), wrap(y + 2) + 1 - 2 * (y % 2), y + 1 - 2 * (y % 2), y))

    def part(j, v, cols):
        return flat.at[j, pl.ds(pl.multiple_of(v * ROWS, 32), ROWS), cols]

    def send1(axis, kind, i, value):
        encode(s1buf.at[axis, kind, i], value)
        msg1(axis, kind, i).start()

    dims = (((0,), (0,)), ((), ()))

    def dot(h, g):
        return lax.dot_general(h, g, dims, preferred_element_type=jnp.float32)

    def ahead(k):
        return 1 if (k & 1) == 0 else -1

    def send_b1(j):
        send1(1, 0, j, part(j, wrap(y + 2), cols(1))[...])

    def send_b2(j):
        send1(1, 1, j, part(j, wrap(y - way(j)), cols(1))[...])

    def send_a(i, carry):
        send1(0, 0, i, part(0, y_of(i), cols(0))[...])
        return carry

    load_g.wait()
    load_h(0).wait()
    flat[0] = dot(h_own[0], g_own[...])
    swap_g.wait_recv()
    swap_near.wait_recv()
    flat[0, near_window, :] += dot(h_par[0, :, near_window], g_par[...])
    send_a(0, 0)
    send_b1(0)
    send_a(1, 0)
    swap_far.wait_recv()
    flat[0, far_window, :] += dot(h_par[0, :, far_window], g_par[...])
    lax.fori_loop(2, N, send_a, 0)
    send_b2(0)
    told(0)
    tell(1)

    def chunk(j, carry):
        load_h(j).wait()
        flat[j] = dot(h_own[j], g_own[...])
        swap_h(j).wait_recv()
        flat[j] += dot(h_par[j], g_par[...])
        send_b1(j)
        send_b2(j)

        @pl.when(j < 3)
        def _():
            def body(m, carry):
                i = 2 * m + 2 - j
                send1(0, 1, i, part(j, y_of(i), cols(0))[...])
                return carry

            lax.fori_loop(0, 2, body, 0)

        return carry

    lax.fori_loop(1, N, chunk, 0)
    told(1)
    tell(2)

    def combine(i, carry):
        for axis in (0, 1):
            msg1(axis, 0, i).wait_recv()
            mid = part(1 + i % 2, y_of(i), cols(0)) if axis == 0 else part(i, wrap(y + way(i)), cols(1))
            send1(axis, 2, i, mid[...] + decode(r1buf.at[axis, 0, i]))
        return carry

    lax.fori_loop(0, N, combine, 0)

    def mine(k, i):
        return part(3, y_of(i), own(k)) if k < 2 else part(i, y, own(k))

    def beyond(k, lanes):
        if k < 2:
            return part(3, wrap(y + ahead(k)), lanes)
        return part(1 + (k & 1), y, lanes)

    def send2(k, kind, value):
        encode(s2buf.at[k, kind], value)
        msg2(k, kind).start()

    def settle(i, carry):
        for axis in (0, 1):
            msg1(axis, 1, i).wait_recv()
            msg1(axis, 2, i).wait_recv()
            ref = part(3, y_of(i), cols(0)) if axis == 0 else part(i, y, cols(1))
            ref[...] += decode(r1buf.at[axis, 1, i]) + decode(r1buf.at[axis, 2, i])

        @pl.when(i == 0)
        def _():
            for k in range(4):
                send2(k, 0, mine(k, 0)[...])

        @pl.when(i == 2)
        def _():
            for k in range(4):
                send2(k, 1, beyond(k, other(k))[...])

        return carry

    lax.fori_loop(0, N - 1, settle, 0)
    for k in range(4):
        msg2(k, 0).wait_recv()
        send2(k, 2, beyond(k, own(k))[...] + decode(r2buf.at[k, 0]))
    settle(jnp.int32(3), 0)
    told(2)
    for k in range(4):
        msg2(k, 1).wait_recv()
    for k in range(4):
        grad[:, own(k)] = mine(k, 3)[...] + decode(r2buf.at[k ^ 1, 1])
    folded = jnp.zeros((ROWS, H), jnp.float32)
    for k in range(4):
        msg2(k, 2).wait_recv()
        final = grad[:, own(k)] + decode(r2buf.at[k, 2])
        grad[:, own(k)] = final
        folded = folded + (final * final + small_term)

    tall[pl.ds(0, ROWS), :] = folded
    tall[pl.ds(ROWS, 256 - ROWS), :] = jnp.zeros((256 - ROWS, 128), jnp.float32)
    rowx[z] = jnp.sum(tall[...].T, axis=0, keepdims=True)

    def exchange(ref, slot, peers, send, recv):
        copies = [remote(ref.at[slot], ref.at[slot], send.at[n], recv.at[n], peer) for n, peer in enumerate(peers)]
        for copy in copies:
            copy.start()
        return copies

    def arrive(copies):
        for copy in copies:
            copy.wait_recv()
        return copies

    pending = exchange(rowx, z, peers_z, zs, zr)
    for turn in (0, 1):
        for k in range(4):
            early(k, turn).start()
    g = grad[...]
    col_sum = jnp.sum(g * g + small_term, axis=0, keepdims=True)
    for copy in small:
        copy.wait()
    arrive(pending)
    row_total = jnp.sum(rowx[...], axis=0)
    new_rows = decay_rate * rp[...] + (1.0 - decay_rate) * row_total[:, 0:ROWS] / D
    nrow[...] = new_rows
    wide = jnp.concatenate([new_rows, jnp.ones((1, 256 - ROWS), jnp.float32)], axis=1)
    row_scale = jnp.broadcast_to(lax.rsqrt(wide), (128, 256)).T[0:ROWS, :]
    scaled = g * jnp.concatenate([row_scale] * 4, axis=1)

    colc[c, pl.ds(0, 1), :] = col_sum
    colc[c, pl.ds(1, 1), :] = jnp.sum(scaled * scaled, axis=0, keepdims=True)
    across = exchange(colc, c, [partner], cs, cr)

    def code(k):
        return remote(rcode.at[k // 2], rnear.at[k], fs.at[k], fr.at[k], link1[k])

    for axis in (0, 1):
        encode(rcode.at[axis], scaled[:, axis * 2 * H : (axis + 1) * 2 * H])
    pending += arrive(across)
    plane[s] = colc[0] + colc[1]
    around = exchange(plane, s, peers_plane, ps, pr)
    for k in range(4):
        code(k).start()
    pending += arrive(around)
    both = jnp.sum(plane[...], axis=0)
    new_cols = decay_rate * cp[...] + (1.0 - decay_rate) * both[0:1] / FF_WIN
    ncol[...] = new_cols
    ratio = both[1:2] / new_cols
    short = ratio[:, 0:128] + ratio[:, 128:256] + ratio[:, 256:384] + ratio[:, 384:512]
    sizx[z] = short
    last = exchange(sizx, z, peers_z, ss, sr)
    col_scale = lax.rsqrt(new_cols)
    raw = scaled * col_scale

    def side_of(axis):
        return col_scale[:, axis * 2 * H : (axis + 1) * 2 * H]


    for axis in (0, 1):
        down[:, cols(axis)] = decode(rcode.at[axis]) * side_of(axis)
    for k in (0, 2, 1, 3):
        code(k).wait_recv()
        dnear[k] = decode(rnear.at[k]) * side_of(k // 2)
        early(k, 0).wait_recv()
        early(k, 1).wait_recv()
    pending += arrive(last)
    raw_total = jnp.sum(jnp.sum(sizx[...], axis=0), axis=1, keepdims=True)
    size = jnp.sqrt(raw_total / (FF_WIN * D))
    clip = 1.0 / jnp.maximum(1.0, size)

    def fresh(weight, step):
        return (weight - learn_rate * (step * clip)).astype(jnp.bfloat16)

    nw[s] = fresh(mas[...], down[...])

    def block(px, py):
        return wrap(px) * N + wrap(py)

    def pair(k):
        return pl.ds((k // 2) * 2 * H, 2 * H)

    def gather(send, recv, src, cols, peer):
        return remote(nw.at[src, :, cols], nw.at[src, :, cols], send, recv, peer)

    from_link = [block(x - 1, y), block(x + 1, y), block(x, y - 1), block(x, y + 1)]
    opposite = [block(x + 2, y), block(x, y + 2)]

    def direct(k, part_of, src):
        return gather(ws.at[k, part_of], wr.at[k, part_of], src, pl.ds(part_of * 2 * H, 2 * H), link1[k])

    def relay(k, src):
        return gather(bs.at[k], br.at[k], src, pl.ds((k & 1) * 2 * H, 2 * H), link1[k])

    def second(k, n, src):
        return gather(a2s.at[k, n, 0], a2r.at[k, n, 0], src, pair(k), link2[k])

    def beside(k, n):
        step = (-1, 1, 2)[n]
        return block(x + step, y - ahead(k)) if k < 2 else block(x - ahead(k), y + step)

    def third(k, n):
        return gather(a2s.at[k, n, 1], a2r.at[k, n, 1], beside(k, n), own(k), link2[k])

    sends = []

    def go(copy):
        copy.start()
        sends.append(copy)

    for k in (1, 2, 0, 3):
        go(direct(k, 1 - k // 2, s))
    for k in (0, 3, 1, 2):
        nw[from_link[k], :, pair(k)] = fresh(mnear[k], dnear[k])
        if k in (0, 3):
            go(relay(k, from_link[k]))
        for side in (0, 1):
            go(second((k & 2) + side, k & 1, from_link[k]))
    upd[...] = raw * clip
    for k in (1, 2):
        direct(k, 1 - k // 2, from_link[k]).wait_recv()
        go(relay(k, from_link[k]))
    for k, axis in ((0, 0), (3, 1)):
        relay(k, opposite[axis]).wait_recv()
        for side in (0, 1):
            go(second(axis * 2 + side, 2, opposite[axis]))
    for n in range(3):
        for k in range(4):
            second(k, n, beside(k, n)).wait_recv()
            go(third(k, n))
    for k in (0, 3):
        direct(k, 1 - k // 2, from_link[k]).wait_recv()
    relay(1, opposite[0]).wait_recv()
    relay(2, opposite[1]).wait_recv()
    for n in range(3):
        for k in range(4):
            third(k, n).wait_recv()

    for copy in sends + pending + swaps:
        copy.wait_send()
    for k in range(4):
        early(k, 0).wait_send()
        early(k, 1).wait_send()
        code(k).wait_send()

    def drain(i, carry):
        for axis in (0, 1):
            for kind in range(3):
                msg1(axis, kind, i).wait_send()
        return carry

    lax.fori_loop(0, N, drain, 0)
    for k in range(4):
        for kind in range(3):
            msg2(k, kind).wait_send()


def writer(nw, upd, nrow, ncol, nw_out, upd_out, nrow_out, ncol_out, sem):
    quarter = N * N // 4
    pairs = [(nw.at[pl.ds(n * quarter, quarter)], nw_out.at[pl.ds(n * quarter, quarter)]) for n in range(4)]
    pairs += [(upd, upd_out), (nrow, nrow_out), (ncol, ncol_out)]
    copies = [pltpu.make_async_copy(src, dst, sem.at[n]) for n, (src, dst) in enumerate(pairs)]
    for copy in copies:
        copy.start()
    for copy in copies:
        copy.wait()


def per_device(hidden, grad_out, master_weight, row_prev, col_prev):
    hbm = pl.BlockSpec(memory_space=pltpu.HBM)
    vmem = pl.BlockSpec(memory_space=pltpu.VMEM)
    f32, bf16 = jnp.float32, jnp.bfloat16
    dma = pltpu.SemaphoreType.DMA
    results = (((N * N, ROWS, COLS), bf16), ((ROWS, COLS), f32), ((1, ROWS), f32), ((1, COLS), f32))
    held = pl.pallas_call(
        kernel,
        out_shape=tuple(pltpu.VMEM(shape, kind) for shape, kind in results),
        in_specs=[hbm] * 5,
        out_specs=(vmem,) * 4,
        scratch_shapes=[
            pltpu.VMEM((N, TOK, CHUNK), bf16),
            pltpu.VMEM((N, TOK, CHUNK), bf16),
            pltpu.VMEM((TOK, COLS), bf16),
            pltpu.VMEM((TOK, COLS), bf16),
            pltpu.VMEM((N, CHUNK, COLS), f32),
            pltpu.VMEM((2, 3, N, MSG, 2 * H), bf16),
            pltpu.VMEM((2, 3, N, MSG, 2 * H), bf16),
            pltpu.VMEM((4, 3, MSG, H), bf16),
            pltpu.VMEM((4, 3, MSG, H), bf16),
            pltpu.VMEM((ROWS, COLS), f32),
            pltpu.VMEM((ROWS, COLS), f32),
            pltpu.VMEM((1, ROWS), f32),
            pltpu.VMEM((1, COLS), f32),
            pltpu.VMEM((NZ, 1, 256), f32),
            pltpu.VMEM((256, 128), f32),
            pltpu.VMEM((N * N, 2, COLS), f32),
            pltpu.VMEM((2, 2, COLS), f32),
            pltpu.VMEM((NZ, 1, 128), f32),
            pltpu.VMEM((4, ROWS, 2 * H), f32),
            pltpu.VMEM((2, MSG, 2 * H), bf16),
            pltpu.VMEM((4, MSG, 2 * H), bf16),
            pltpu.VMEM((4, ROWS, 2 * H), f32),
            pltpu.VMEM((ROWS, COLS), f32),
            dma((8,)), dma((7,)), dma((7,)),
            dma((2, 3, N)), dma((2, 3, N)), dma((4, 3)), dma((4, 3)),
            dma((NZ - 1,)), dma((NZ - 1,)), dma((1,)), dma((1,)), dma((N * N - 1,)), dma((N * N - 1,)),
            dma((NZ - 1,)), dma((NZ - 1,)),
            dma((4, 2)), dma((4, 2)), dma((4,)), dma((4,)), dma((4, 3, 2)), dma((4, 3, 2)),
            dma((4, 2)), dma((4, 2)), dma((4,)), dma((4,)),
            pltpu.SemaphoreType.REGULAR((3,)),
        ],
        compiler_params=pltpu.CompilerParams(collective_id=0, has_side_effects=True, vmem_limit_bytes=62700000),
    )(hidden, grad_out, master_weight, row_prev.reshape(1, ROWS), col_prev.reshape(1, COLS))
    nw, upd, nrows, ncols = pl.pallas_call(
        writer,
        out_shape=tuple(jax.ShapeDtypeStruct(shape, kind) for shape, kind in results),
        in_specs=[vmem] * 4,
        out_specs=(hbm,) * 4,
        scratch_shapes=[dma((7,))],
        compiler_params=pltpu.CompilerParams(vmem_limit_bytes=1024 * 1024),
    )(*held)
    return nw.reshape(HALF, COLS), upd, nrows.reshape(ROWS), ncols.reshape(COLS)


def solution(mesh):
    return jax.shard_map(
        per_device,
        mesh=mesh,
        in_specs=(
            P(("dp", "seq"), None),
            P(("dp", "seq"), "tensor"),
            P(("dp", "seq"), "tensor"),
            P(("dp", "seq")),
            P("tensor"),
        ),
        out_specs=(P("dp", "tensor"), P(("dp", "seq"), "tensor"), P(("dp", "seq")), P("tensor")),
        check_vma=False,
    )
```

```python
import jax
import jax.numpy as jnp
from jax import lax
from jax.experimental import pallas as pl
from jax.experimental.pallas import tpu as pltpu
from jax.sharding import PartitionSpec as P

D = 4096
FF_WIN = 7168
decay_rate = 0.8
learn_rate = 0.05
small_term = 1e-06

N = 4
NZ = 8
TOK = 512
ROWS = 224
COLS = 512
HALF = FF_WIN // 2
CHUNK = HALF // N
H = 128
G = 8
MSG = ROWS + G
POWER = 9.0
TOP = 15000.0
OFFS = (2, 1, 3, 0)
MESH = pl.DeviceIdType.MESH


def pick(i, values):
    out = values[-1]
    for n in range(len(values) - 2, -1, -1):
        out = jnp.where(i == n, values[n], out)
    return out


def encode(ref, value):
    groups = value.reshape(ROWS // G, G, value.shape[1])
    peak = jnp.maximum(jnp.max(jnp.abs(groups), axis=0), 1e-30).astype(jnp.bfloat16)
    scale = TOP / peak.astype(jnp.float32)
    u = groups * scale[None]
    u2 = u * u
    u4 = u2 * u2
    u8 = u4 * u4
    ref[pl.ds(0, ROWS), :] = (u8 * u).astype(jnp.bfloat16).reshape(value.shape)
    ref[pl.ds(ROWS, G), :] = peak


def decode(ref):
    width = ref.shape[1]
    code = ref[pl.ds(0, ROWS), :].astype(jnp.float32).reshape(ROWS // G, G, width)
    scale = ref[pl.ds(ROWS, G), :].astype(jnp.float32) * (1.0 / TOP)
    size = jnp.exp(jnp.log(jnp.maximum(jnp.abs(code), 1.2e-38)) * (1.0 / POWER))
    return (size * jnp.where(code < 0.0, -scale[None], scale[None])).reshape(ROWS, width)


def kernel(
    hid, gout, master, rprev, cprev,
    nw, upd, nrow, ncol,
    h_own, h_par, g_own, g_par, flat, s1buf, r1buf, s2buf, r2buf, grad, mas, rp, cp,
    rowx, tall, plane, colc, sizx, mnear, rcode, rnear, dnear, down,
    ld_sem, xs_sem, xr_sem, s1s, r1s, s2s, r2s, zs, zr, cs, cr, ps, pr, ss, sr, ws, wr, bs, br, a2s, a2r, es, er, fs, fr, chain,
):
    c = lax.axis_index("dp")
    s = lax.axis_index("seq")
    z = lax.axis_index("tensor")
    x = s // N
    y = s % N

    def wrap(v):
        return lax.rem(v + N, N)

    def at(px, py):
        return (c, wrap(px) * N + wrap(py), z)

    partner = (1 - c, s, z)
    steps = sorted(range(1, N * N), key=lambda d: -min(d // N, N - d // N) - min(d % N, N - d % N))
    peers_plane = [at(x + d // N, y + d % N) for d in steps]
    peers_z = [(c, s, lax.rem(z + d, NZ)) for d in (4, 3, 5, 2, 6, 1, 7)]
    right_x, left_x = at(x + 1, y), at(x - 1, y)
    right_y, left_y = at(x, y + 1), at(x, y - 1)
    link1 = [right_x, left_x, right_y, left_y]
    link2 = [right_y, left_y, right_x, left_x]
    near = link1 + peers_z[-2:]

    barrier = pltpu.get_barrier_semaphore()
    for peer in [partner] + near:
        pl.semaphore_signal(barrier, inc=1, device_id=peer, device_id_type=MESH)

    first = 1 - y // 2
    near_window = pl.ds(pl.multiple_of(first * 384, 128), 512)
    far_window = pl.ds(pl.multiple_of((1 - first) * 512, 128), 384)

    def start_of(core, j):
        return core * HALF + wrap(x + pick(j, OFFS)) * CHUNK

    def columns(core, j):
        return pl.ds(pl.multiple_of(start_of(core, j), 128), CHUNK)

    def load(src, dst, n):
        return pltpu.make_async_copy(src, dst, ld_sem.at[n])

    def load_h(j):
        return load(hid.at[:, columns(c, j)], h_own.at[j], j)

    load_g = load(gout, g_own, 4)
    small = [load(master, mas, 5), load(rprev, rp, 6), load(cprev, cp, 7)]
    load_g.start()
    for j in range(N):
        load_h(j).start()
    pl.semaphore_wait(barrier, 1 + len(near))

    def remote(src, dst, send, recv, peer):
        return pltpu.make_async_remote_copy(
            src_ref=src, dst_ref=dst, send_sem=send, recv_sem=recv, device_id=peer, device_id_type=MESH
        )

    def tell(n):
        for peer in near:
            pl.semaphore_signal(chain.at[n], inc=1, device_id=peer, device_id_type=MESH)

    def told(n):
        pl.semaphore_wait(chain.at[n], len(near))

    base = start_of(1 - c, 0)
    src_near = pl.ds(pl.multiple_of(base + first * 384, 128), 512)
    src_far = pl.ds(pl.multiple_of(base + (1 - first) * 512, 128), 384)

    def swap(n, src, dst):
        return remote(src, dst, xs_sem.at[n], xr_sem.at[n], partner)

    def swap_h(j):
        return swap(j, hid.at[:, columns(1 - c, j)], h_par.at[j])

    swap_near = swap(0, hid.at[:, src_near], h_par.at[0, :, near_window])
    swap_far = swap(6, hid.at[:, src_far], h_par.at[0, :, far_window])
    swap_g = swap(4, gout, g_par)
    swaps = [swap_g, swap_near, swap_far] + [swap_h(j) for j in range(1, N)]
    for copy in swaps:
        copy.start()
    for copy in small:
        copy.start()

    def early(k, turn):
        rows = pl.ds(turn * (ROWS // 2), ROWS // 2)
        lanes = pl.ds((k // 2) * 2 * H, 2 * H)
        return remote(master.at[rows, lanes], mnear.at[k, rows], es.at[k, turn], er.at[k, turn], link1[k])

    tell(0)

    def way(i):
        return 1 - 2 * (i % 2)

    def cols(axis):
        return pl.ds(axis * 2 * H, 2 * H)

    def msg1(axis, kind, i):
        step = -way(i) if kind == 1 else way(i)
        peer = at(x + step, y) if axis == 0 else at(x, y + step)
        index = (axis, kind, i)
        return remote(s1buf.at[index], r1buf.at[index], s1s.at[index], r1s.at[index], peer)

    def msg2(k, kind):
        return remote(s2buf.at[k, kind], r2buf.at[k, kind], s2s.at[k, kind], r2s.at[k, kind], link2[k])

    def own(k):
        return pl.ds(k * H, H)

    def other(k):
        return pl.ds((k ^ 1) * H, H)

    def y_of(i):
        return pick(i, (wrap(y + 2), wrap(y + 2) + 1 - 2 * (y % 2), y + 1 - 2 * (y % 2), y))

    def part(j, v, cols):
        return flat.at[j, pl.ds(pl.multiple_of(v * ROWS, 32), ROWS), cols]

    def send1(axis, kind, i, value):
        encode(s1buf.at[axis, kind, i], value)
        msg1(axis, kind, i).start()

    dims = (((0,), (0,)), ((), ()))

    def dot(h, g):
        return lax.dot_general(h, g, dims, preferred_element_type=jnp.float32)

    def ahead(k):
        return 1 if (k & 1) == 0 else -1

    def send_b1(j):
        send1(1, 0, j, part(j, wrap(y + 2), cols(1))[...])

    def send_b2(j):
        send1(1, 1, j, part(j, wrap(y - way(j)), cols(1))[...])

    def send_a(i, carry):
        send1(0, 0, i, part(0, y_of(i), cols(0))[...])
        return carry

    load_g.wait()
    load_h(0).wait()
    flat[0] = dot(h_own[0], g_own[...])
    swap_g.wait_recv()
    swap_near.wait_recv()
    flat[0, near_window, :] += dot(h_par[0, :, near_window], g_par[...])
    send_a(0, 0)
    send_b1(0)
    send_a(1, 0)
    swap_far.wait_recv()
    flat[0, far_window, :] += dot(h_par[0, :, far_window], g_par[...])
    lax.fori_loop(2, N, send_a, 0)
    send_b2(0)
    told(0)
    tell(1)

    def chunk(j, carry):
        load_h(j).wait()
        flat[j] = dot(h_own[j], g_own[...])
        swap_h(j).wait_recv()
        flat[j] += dot(h_par[j], g_par[...])
        send_b1(j)
        send_b2(j)

        @pl.when(j < 3)
        def _():
            def body(m, carry):
                i = 2 * m + 2 - j
                send1(0, 1, i, part(j, y_of(i), cols(0))[...])
                return carry

            lax.fori_loop(0, 2, body, 0)

        return carry

    lax.fori_loop(1, N, chunk, 0)
    told(1)
    tell(2)

    def combine(i, carry):
        for axis in (0, 1):
            msg1(axis, 0, i).wait_recv()
            mid = part(1 + i % 2, y_of(i), cols(0)) if axis == 0 else part(i, wrap(y + way(i)), cols(1))
            send1(axis, 2, i, mid[...] + decode(r1buf.at[axis, 0, i]))
        return carry

    lax.fori_loop(0, N, combine, 0)

    def mine(k, i):
        return part(3, y_of(i), own(k)) if k < 2 else part(i, y, own(k))

    def beyond(k, lanes):
        if k < 2:
            return part(3, wrap(y + ahead(k)), lanes)
        return part(1 + (k & 1), y, lanes)

    def send2(k, kind, value):
        encode(s2buf.at[k, kind], value)
        msg2(k, kind).start()

    def settle(i, carry):
        for axis in (0, 1):
            msg1(axis, 1, i).wait_recv()
            msg1(axis, 2, i).wait_recv()
            ref = part(3, y_of(i), cols(0)) if axis == 0 else part(i, y, cols(1))
            ref[...] += decode(r1buf.at[axis, 1, i]) + decode(r1buf.at[axis, 2, i])

        @pl.when(i == 0)
        def _():
            for k in range(4):
                send2(k, 0, mine(k, 0)[...])

        @pl.when(i == 2)
        def _():
            for k in range(4):
                send2(k, 1, beyond(k, other(k))[...])

        return carry

    lax.fori_loop(0, N - 1, settle, 0)
    for k in range(4):
        msg2(k, 0).wait_recv()
        send2(k, 2, beyond(k, own(k))[...] + decode(r2buf.at[k, 0]))
    settle(jnp.int32(3), 0)
    told(2)
    for k in range(4):
        msg2(k, 1).wait_recv()
    for k in range(4):
        grad[:, own(k)] = mine(k, 3)[...] + decode(r2buf.at[k ^ 1, 1])
    folded = jnp.zeros((ROWS, H), jnp.float32)
    for k in range(4):
        msg2(k, 2).wait_recv()
        final = grad[:, own(k)] + decode(r2buf.at[k, 2])
        grad[:, own(k)] = final
        folded = folded + (final * final + small_term)

    tall[pl.ds(0, ROWS), :] = folded
    tall[pl.ds(ROWS, 256 - ROWS), :] = jnp.zeros((256 - ROWS, 128), jnp.float32)
    rowx[z] = jnp.sum(tall[...].T, axis=0, keepdims=True)

    def exchange(ref, slot, peers, send, recv):
        copies = [remote(ref.at[slot], ref.at[slot], send.at[n], recv.at[n], peer) for n, peer in enumerate(peers)]
        for copy in copies:
            copy.start()
        return copies

    def arrive(copies):
        for copy in copies:
            copy.wait_recv()
        return copies

    pending = exchange(rowx, z, peers_z, zs, zr)
    for turn in (0, 1):
        for k in range(4):
            early(k, turn).start()
    g = grad[...]
    col_sum = jnp.sum(g * g + small_term, axis=0, keepdims=True)
    for copy in small:
        copy.wait()
    arrive(pending)
    row_total = jnp.sum(rowx[...], axis=0)
    new_rows = decay_rate * rp[...] + (1.0 - decay_rate) * row_total[:, 0:ROWS] / D
    nrow[...] = new_rows
    wide = jnp.concatenate([new_rows, jnp.ones((1, 256 - ROWS), jnp.float32)], axis=1)
    row_scale = jnp.broadcast_to(lax.rsqrt(wide), (128, 256)).T[0:ROWS, :]
    scaled = g * jnp.concatenate([row_scale] * 4, axis=1)

    colc[c, pl.ds(0, 1), :] = col_sum
    colc[c, pl.ds(1, 1), :] = jnp.sum(scaled * scaled, axis=0, keepdims=True)
    across = exchange(colc, c, [partner], cs, cr)

    def code(k):
        return remote(rcode.at[k // 2], rnear.at[k], fs.at[k], fr.at[k], link1[k])

    for axis in (0, 1):
        encode(rcode.at[axis], scaled[:, axis * 2 * H : (axis + 1) * 2 * H])
    pending += arrive(across)
    plane[s] = colc[0] + colc[1]
    around = exchange(plane, s, peers_plane, ps, pr)
    for k in range(4):
        code(k).start()
    pending += arrive(around)
    both = jnp.sum(plane[...], axis=0)
    new_cols = decay_rate * cp[...] + (1.0 - decay_rate) * both[0:1] / FF_WIN
    ncol[...] = new_cols
    ratio = both[1:2] / new_cols
    short = ratio[:, 0:128] + ratio[:, 128:256] + ratio[:, 256:384] + ratio[:, 384:512]
    sizx[z] = short
    last = exchange(sizx, z, peers_z, ss, sr)
    col_scale = lax.rsqrt(new_cols)
    raw = scaled * col_scale

    def side_of(axis):
        return col_scale[:, axis * 2 * H : (axis + 1) * 2 * H]


    for axis in (0, 1):
        down[:, cols(axis)] = decode(rcode.at[axis]) * side_of(axis)
    for k in (0, 2, 1, 3):
        code(k).wait_recv()
        dnear[k] = decode(rnear.at[k]) * side_of(k // 2)
        early(k, 0).wait_recv()
        early(k, 1).wait_recv()
    pending += arrive(last)
    raw_total = jnp.sum(jnp.sum(sizx[...], axis=0), axis=1, keepdims=True)
    size = jnp.sqrt(raw_total / (FF_WIN * D))
    clip = 1.0 / jnp.maximum(1.0, size)

    def fresh(weight, step):
        return (weight - learn_rate * (step * clip)).astype(jnp.bfloat16)

    nw[s] = fresh(mas[...], down[...])

    def block(px, py):
        return wrap(px) * N + wrap(py)

    def pair(k):
        return pl.ds((k // 2) * 2 * H, 2 * H)

    def gather(send, recv, src, cols, peer):
        return remote(nw.at[src, :, cols], nw.at[src, :, cols], send, recv, peer)

    from_link = [block(x - 1, y), block(x + 1, y), block(x, y - 1), block(x, y + 1)]
    opposite = [block(x + 2, y), block(x, y + 2)]

    def direct(k, part_of, src):
        return gather(ws.at[k, part_of], wr.at[k, part_of], src, pl.ds(part_of * 2 * H, 2 * H), link1[k])

    def relay(k, src):
        return gather(bs.at[k], br.at[k], src, pl.ds((k & 1) * 2 * H, 2 * H), link1[k])

    def second(k, n, src):
        return gather(a2s.at[k, n, 0], a2r.at[k, n, 0], src, pair(k), link2[k])

    def beside(k, n):
        step = (-1, 1, 2)[n]
        return block(x + step, y - ahead(k)) if k < 2 else block(x - ahead(k), y + step)

    def third(k, n):
        return gather(a2s.at[k, n, 1], a2r.at[k, n, 1], beside(k, n), own(k), link2[k])

    sends = []

    def go(copy):
        copy.start()
        sends.append(copy)

    for k in (1, 2, 0, 3):
        go(direct(k, 1 - k // 2, s))
    for k in (0, 3, 1, 2):
        nw[from_link[k], :, pair(k)] = fresh(mnear[k], dnear[k])
        if k in (0, 3):
            go(relay(k, from_link[k]))
        for side in (0, 1):
            go(second((k & 2) + side, k & 1, from_link[k]))
    upd[...] = raw * clip
    for k in (1, 2):
        direct(k, 1 - k // 2, from_link[k]).wait_recv()
        go(relay(k, from_link[k]))
    for k, axis in ((0, 0), (3, 1)):
        relay(k, opposite[axis]).wait_recv()
        for side in (0, 1):
            go(second(axis * 2 + side, 2, opposite[axis]))
    for n in range(3):
        for k in range(4):
            second(k, n, beside(k, n)).wait_recv()
            go(third(k, n))
    for k in (0, 3):
        direct(k, 1 - k // 2, from_link[k]).wait_recv()
    relay(1, opposite[0]).wait_recv()
    relay(2, opposite[1]).wait_recv()
    for n in range(3):
        for k in range(4):
            third(k, n).wait_recv()

    for copy in sends + pending + swaps:
        copy.wait_send()
    for k in range(4):
        early(k, 0).wait_send()
        early(k, 1).wait_send()
        code(k).wait_send()

    def drain(i, carry):
        for axis in (0, 1):
            for kind in range(3):
                msg1(axis, kind, i).wait_send()
        return carry

    lax.fori_loop(0, N, drain, 0)
    for k in range(4):
        for kind in range(3):
            msg2(k, kind).wait_send()


def writer(nw, upd, nrow, ncol, nw_out, upd_out, nrow_out, ncol_out, sem):
    quarter = N * N // 4
    pairs = [(nw.at[pl.ds(n * quarter, quarter)], nw_out.at[pl.ds(n * quarter, quarter)]) for n in range(4)]
    pairs += [(upd, upd_out), (nrow, nrow_out), (ncol, ncol_out)]
    copies = [pltpu.make_async_copy(src, dst, sem.at[n]) for n, (src, dst) in enumerate(pairs)]
    for copy in copies:
        copy.start()
    for copy in copies:
        copy.wait()


def per_device(hidden, grad_out, master_weight, row_prev, col_prev):
    hbm = pl.BlockSpec(memory_space=pltpu.HBM)
    vmem = pl.BlockSpec(memory_space=pltpu.VMEM)
    f32, bf16 = jnp.float32, jnp.bfloat16
    dma = pltpu.SemaphoreType.DMA
    results = (((N * N, ROWS, COLS), bf16), ((ROWS, COLS), f32), ((1, ROWS), f32), ((1, COLS), f32))
    held = pl.pallas_call(
        kernel,
        out_shape=tuple(pltpu.VMEM(shape, kind) for shape, kind in results),
        in_specs=[hbm] * 5,
        out_specs=(vmem,) * 4,
        scratch_shapes=[
            pltpu.VMEM((N, TOK, CHUNK), bf16),
            pltpu.VMEM((N, TOK, CHUNK), bf16),
            pltpu.VMEM((TOK, COLS), bf16),
            pltpu.VMEM((TOK, COLS), bf16),
            pltpu.VMEM((N, CHUNK, COLS), f32),
            pltpu.VMEM((2, 3, N, MSG, 2 * H), bf16),
            pltpu.VMEM((2, 3, N, MSG, 2 * H), bf16),
            pltpu.VMEM((4, 3, MSG, H), bf16),
            pltpu.VMEM((4, 3, MSG, H), bf16),
            pltpu.VMEM((ROWS, COLS), f32),
            pltpu.VMEM((ROWS, COLS), f32),
            pltpu.VMEM((1, ROWS), f32),
            pltpu.VMEM((1, COLS), f32),
            pltpu.VMEM((NZ, 1, 256), f32),
            pltpu.VMEM((256, 128), f32),
            pltpu.VMEM((N * N, 2, COLS), f32),
            pltpu.VMEM((2, 2, COLS), f32),
            pltpu.VMEM((NZ, 1, 128), f32),
            pltpu.VMEM((4, ROWS, 2 * H), f32),
            pltpu.VMEM((2, MSG, 2 * H), bf16),
            pltpu.VMEM((4, MSG, 2 * H), bf16),
            pltpu.VMEM((4, ROWS, 2 * H), f32),
            pltpu.VMEM((ROWS, COLS), f32),
            dma((8,)), dma((7,)), dma((7,)),
            dma((2, 3, N)), dma((2, 3, N)), dma((4, 3)), dma((4, 3)),
            dma((NZ - 1,)), dma((NZ - 1,)), dma((1,)), dma((1,)), dma((N * N - 1,)), dma((N * N - 1,)),
            dma((NZ - 1,)), dma((NZ - 1,)),
            dma((4, 2)), dma((4, 2)), dma((4,)), dma((4,)), dma((4, 3, 2)), dma((4, 3, 2)),
            dma((4, 2)), dma((4, 2)), dma((4,)), dma((4,)),
            pltpu.SemaphoreType.REGULAR((3,)),
        ],
        compiler_params=pltpu.CompilerParams(collective_id=0, has_side_effects=True, vmem_limit_bytes=62700000),
    )(hidden, grad_out, master_weight, row_prev.reshape(1, ROWS), col_prev.reshape(1, COLS))
    nw, upd, nrows, ncols = pl.pallas_call(
        writer,
        out_shape=tuple(jax.ShapeDtypeStruct(shape, kind) for shape, kind in results),
        in_specs=[vmem] * 4,
        out_specs=(hbm,) * 4,
        scratch_shapes=[dma((7,))],
        compiler_params=pltpu.CompilerParams(vmem_limit_bytes=1024 * 1024),
    )(*held)
    return nw.reshape(HALF, COLS), upd, nrows.reshape(ROWS), ncols.reshape(COLS)


def solution(mesh):
    return jax.shard_map(
        per_device,
        mesh=mesh,
        in_specs=(
            P(("dp", "seq"), None),
            P(("dp", "seq"), "tensor"),
            P(("dp", "seq"), "tensor"),
            P(("dp", "seq")),
            P("tensor"),
        ),
        out_specs=(P("dp", "tensor"), P(("dp", "seq"), "tensor"), P(("dp", "seq")), P("tensor")),
        check_vma=False,
    )
```
